32 devices in a mesh: seq: 2 (over x), head: 4 (over y, core), fsdp: 4 (over z).
Axes of the slice: x: 2, y: 2, z: 4, core: 2. Of those that a mesh axis runs over, the one named last changes fastest.
Arguments:
- block_input: bfloat16 [3, 4, 1024, 1024], P(None, 'fsdp', 'seq'), may hold values from -6 to 6
- cotangent: bfloat16 [3, 4, 1024, 1024], P(None, 'fsdp', 'seq'), may hold values from -6 to 6
- doc_lengths: int32 [3, 4, 8], P(None, 'fsdp'), may hold values from 1 to 512, as said below
- attn_gain: float32 [1024], replicated, may hold values from 0.25 to 1.75
- w_query: bfloat16 [1024, 1024], P('fsdp', 'head'), may hold values from -0.1875 to 0.1875
- w_key: bfloat16 [1024, 1024], P('fsdp', 'head'), may hold values from -0.1875 to 0.1875
- w_value: bfloat16 [1024, 2048], P('fsdp', 'head'), may hold values from -0.1875 to 0.1875
- w_gate: bfloat16 [1024, 2048], P('fsdp', 'head'), may hold values from -0.1875 to 0.1875
- w_alpha: bfloat16 [1024, 8], P('fsdp', 'head'), may hold values from -0.1875 to 0.1875
- w_beta: bfloat16 [1024, 8], P('fsdp', 'head'), may hold values from -0.1875 to 0.1875
- conv_query: float32 [4, 1024], replicated, may hold values from -3 to 3
- conv_key: float32 [4, 1024], replicated, may hold values from -3 to 3
- conv_value: float32 [4, 2048], replicated, may hold values from -3 to 3
- a_log: float32 [8], replicated, may hold values from -6 to 0
- dt_bias: float32 [8], replicated, may hold values from -3 to -1
- head_gain: float32 [256], replicated, may hold values from 0.25 to 1.75
- w_out: bfloat16 [2048, 1024], P('head', 'fsdp'), may hold values from -0.125 to 0.125
- mlp_gain: float32 [1024], replicated, may hold values from 0.25 to 1.75
- w_ffgate: bfloat16 [1024, 2816], P('fsdp', 'head'), may hold values from -0.1875 to 0.1875
- w_ffup: bfloat16 [1024, 2816], P('fsdp', 'head'), may hold values from -0.1875 to 0.1875
- w_down: bfloat16 [2816, 1024], P('head', 'fsdp'), may hold values from -0.109375 to 0.109375
Outputs:
- block_output: bfloat16 [3, 4, 1024, 1024], P(None, 'fsdp', ('seq', 'head'))
- input_grad: float32 [3, 4, 1024, 1024], P(None, 'fsdp', ('seq', 'head'))
- grad_w_query: float32 [1024, 1024], P(('seq', 'fsdp'), 'head')
- grad_w_key: float32 [1024, 1024], P(('seq', 'fsdp'), 'head')
- grad_w_value: float32 [1024, 2048], P(('seq', 'fsdp'), 'head')
- grad_w_gate: float32 [1024, 2048], P(('seq', 'fsdp'), 'head')
- grad_w_alpha: float32 [1024, 8], P(('seq', 'fsdp'), 'head')
- grad_w_beta: float32 [1024, 8], P(('seq', 'fsdp'), 'head')
- grad_w_out: float32 [2048, 1024], P('head', ('seq', 'fsdp'))
- grad_w_ffgate: float32 [1024, 2816], P(('seq', 'fsdp'), 'head')
- grad_w_ffup: float32 [1024, 2816], P(('seq', 'fsdp'), 'head')
- grad_w_down: float32 [2816, 1024], P('head', ('seq', 'fsdp'))
- grad_attn_gain: float32 [1024], replicated
- grad_mlp_gain: float32 [1024], replicated
- grad_head_gain: float32 [256], replicated
- grad_conv_query: float32 [4, 1024], replicated
- grad_conv_key: float32 [4, 1024], replicated
- grad_conv_value: float32 [4, 2048], replicated
- grad_a_log: float32 [8], replicated
- grad_dt_bias: float32 [8], replicated
The draws below stay inside these ranges and needn't reach their ends.
Inputs may be any that keep to these rules, and one draw needn't show every extreme that they name: `doc_lengths`: each row holds the 8 document lengths of one sequence in order, summing to 1024. Exactly one document, never the first or the last, has 512 tokens; the others share 512 tokens.
All inputs are finite; a program needn't handle non-finite values.
Results may differ from the reference program's by a relative error of at most 0.014.
Values may be sent and summed in bfloat16 or wider, within the bound.
No kernel may reach another device: no remote copies, remote signals or barrier semaphores. Data moves between devices by JAX's collectives and lax.ppermute only.
A program may use at most 256 MiB of HBM per device.

```python
import math
import jax
import jax.numpy as jnp
from jax import lax

D = 1024
H = 8
DK = 128
DV = 256
FF = 2816
KCONV = 4
STRETCH = 64
NDOC = 8
MB = 3
BATCH = 4
SEQ_LEN = 1024
TOK_DEV = 512
HK = 1024
HV = 2048


def draw_doc_lengths(key, part):
    row_total = MB * BATCH
    row_keys = jax.random.split(key, row_total)

    def one_row(row_key):
        cut_key, place_key = jax.random.split(row_key)
        order = jax.random.permutation(cut_key, TOK_DEV - 1) + 1
        cuts = jnp.sort(order[:NDOC - 2]).astype(jnp.int32)
        bounds = jnp.concatenate([jnp.zeros((1,), jnp.int32), cuts, jnp.full((1,), TOK_DEV, jnp.int32)])
        small_docs = bounds[1:] - bounds[:-1]
        place = jax.random.randint(place_key, (), 1, NDOC - 1)
        slots = jnp.arange(NDOC)
        before = small_docs[jnp.clip(slots, 0, NDOC - 2)]
        after = small_docs[jnp.clip(slots - 1, 0, NDOC - 2)]
        lengths = jnp.where(slots < place, before, jnp.where(slots == place, SEQ_LEN - TOK_DEV, after))
        return lengths.astype(jnp.int32)
    return jax.vmap(one_row)(row_keys).reshape(MB, BATCH, NDOC)


def block_scale(own_key, extent, cuts, low, high):
    level = 1.0
    for axis_at, parts in cuts:
        steps = jax.random.uniform(jax.random.fold_in(jax.random.fold_in(own_key, 6), axis_at), (parts,), jnp.float32, low / len(cuts), high / len(cuts))
        level = level * jnp.repeat(jnp.exp(steps), extent[axis_at] // parts).reshape((-1,) + (1,) * (len(extent) - 1 - axis_at))
    return level


def centred(rng, shape, scale, bound, cuts=(), held_as=jnp.bfloat16):
    loudness = block_scale(rng, shape, cuts, -0.22, 0.18) if cuts else 1.0
    entries = jax.random.normal(rng, shape, jnp.float32) * scale * loudness
    return jnp.minimum(jnp.maximum(entries, -bound), bound).astype(held_as)


def setup_inputs(seed: int = 0) -> dict:
    seeds = jax.random.split(jax.random.key(seed), 22)
    return {
        "block_input": centred(seeds[0], (MB, BATCH, SEQ_LEN, D), 1.0, 6.0, ((1, 4), (2, 2))),
        "cotangent": centred(seeds[1], (MB, BATCH, SEQ_LEN, D), 1.0, 6.0, ((1, 4), (2, 2))),
        "doc_lengths": draw_doc_lengths(jax.random.fold_in(seeds[21], 71), 0),
        "attn_gain": jnp.clip(1.0 + 0.15 * jax.random.normal(seeds[3], (D,), jnp.float32), 0.25, 1.75),
        "w_query": centred(seeds[4], (D, HK), D ** -0.5, 0.1875, ((0, 4), (1, 4))),
        "w_key": centred(seeds[5], (D, HK), D ** -0.5, 0.1875, ((0, 4), (1, 4))),
        "w_value": centred(seeds[6], (D, HV), D ** -0.5, 0.1875, ((0, 4), (1, 4))),
        "w_gate": centred(seeds[7], (D, HV), D ** -0.5, 0.1875, ((0, 4), (1, 4))),
        "w_alpha": centred(seeds[8], (D, H), D ** -0.5, 0.1875, ((0, 4), (1, 4))),
        "w_beta": centred(seeds[9], (D, H), D ** -0.5, 0.1875, ((0, 4), (1, 4))),
        "conv_query": centred(seeds[10], (KCONV, HK), 0.5, 3.0, (), jnp.float32),
        "conv_key": centred(seeds[11], (KCONV, HK), 0.5, 3.0, (), jnp.float32),
        "conv_value": centred(seeds[12], (KCONV, HV), 0.5, 3.0, (), jnp.float32),
        "a_log": jnp.clip(jax.random.uniform(seeds[13], (H,), jnp.float32, -6.0, 0.0), -6.0, 0.0),
        "dt_bias": jnp.clip(jax.random.uniform(seeds[14], (H,), jnp.float32, -3.0, -1.0), -3.0, -1.0),
        "head_gain": jnp.clip(1.0 + 0.15 * jax.random.normal(seeds[15], (DV,), jnp.float32), 0.25, 1.75),
        "w_out": centred(seeds[16], (HV, D), HV ** -0.5, 0.125, ((0, 4), (1, 4))),
        "mlp_gain": jnp.clip(1.0 + 0.15 * jax.random.normal(seeds[17], (D,), jnp.float32), 0.25, 1.75),
        "w_ffgate": centred(seeds[18], (D, FF), D ** -0.5, 0.1875, ((0, 4), (1, 4))),
        "w_ffup": centred(seeds[19], (D, FF), D ** -0.5, 0.1875, ((0, 4), (1, 4))),
        "w_down": centred(seeds[20], (FF, D), FF ** -0.5, 0.109375, ((0, 4), (1, 4))),
    }


BEST_PRECISION = lax.Precision.HIGHEST

@jax.custom_vjp
def low(v):
    return lax.optimization_barrier(v.astype(jnp.bfloat16)).astype(jnp.float32)

@jax.custom_vjp
def low_back(v):
    return v

def low_keep(v):
    return (low(v), None)

def low_pass(kept, grad):
    return (grad,)

def back_keep(v):
    return (v, None)

def back_low(kept, grad):
    return (low(grad),)
low.defvjp(low_keep, low_pass)
low_back.defvjp(back_keep, back_low)

def rms_rows(values, gain_vec):
    return values * lax.rsqrt(lax.optimization_barrier(jnp.mean(values * values, axis=-1, keepdims=True)) + 1e-05) * gain_vec

def l2_rows(values):
    return values * lax.rsqrt(lax.optimization_barrier(jnp.sum(values * values, axis=-1, keepdims=True)) + 1e-06)

def short_conv(padded, filters, doc_pad):
    tok_count = padded.shape[0] - KCONV + 1
    own_doc = doc_pad[KCONV - 1:]
    total = jnp.zeros((tok_count, padded.shape[1]), jnp.float32)
    for offset in range(KCONV):
        window = padded[offset:offset + tok_count]
        keep_mask = (doc_pad[offset:offset + tok_count] == own_doc)[:, None]
        total = total + jnp.where(keep_mask, window, 0.0) * filters[offset]
    return jax.nn.silu(total)

def mixer_inputs(q_pad, k_pad, v_pad, alpha_logit, beta_logit, conv_q, conv_k, conv_v, alog_vec, bias_vec, doc_pad):
    tok_count = alpha_logit.shape[0]
    head_count = alpha_logit.shape[1]
    q_conv = short_conv(q_pad, conv_q, doc_pad).reshape(tok_count, head_count, DK)
    k_conv = short_conv(k_pad, conv_k, doc_pad).reshape(tok_count, head_count, DK)
    v_conv = short_conv(v_pad, conv_v, doc_pad).reshape(tok_count, head_count, DV)
    queries = l2_rows(q_conv) * (1.0 / math.sqrt(DK))
    key_vecs = l2_rows(k_conv)
    beta_rate = jax.nn.sigmoid(beta_logit)
    log_decay = -jnp.exp(alog_vec) * jax.nn.softplus(alpha_logit + bias_vec)
    return (queries, key_vecs, v_conv, beta_rate, log_decay)

def stretch_step(running, block_in):
    state_mat, prior_doc = running
    queries, key_vecs, value_vecs, beta_rate, log_decay, doc_ids = block_in
    block_len = queries.shape[0]
    cumulative = jnp.cumsum(log_decay)
    row_ids = jnp.arange(block_len)[:, None]
    col_ids = jnp.arange(block_len)[None, :]
    same_doc = doc_ids[:, None] == doc_ids[None, :]
    decay_mat = jnp.where(same_doc & (row_ids >= col_ids), jnp.exp(jnp.minimum(cumulative[:, None] - cumulative[None, :], 0.0)), 0.0)
    reach = jnp.where(doc_ids == prior_doc, jnp.exp(cumulative), 0.0)
    strict_mat = jnp.where(row_ids > col_ids, decay_mat, 0.0)
    key_gram = jnp.dot(key_vecs, key_vecs.T, precision=BEST_PRECISION)
    lower_mat = jnp.eye(block_len, dtype=jnp.float32) + beta_rate[:, None] * strict_mat * key_gram
    from_state = jnp.dot(key_vecs, state_mat, precision=BEST_PRECISION)
    pseudo = jax.scipy.linalg.solve_triangular(lower_mat, beta_rate[:, None] * (value_vecs - reach[:, None] * from_state), lower=True, unit_diagonal=True)
    scores = jnp.dot(queries, key_vecs.T, precision=BEST_PRECISION)
    outputs = reach[:, None] * jnp.dot(queries, state_mat, precision=BEST_PRECISION) + jnp.dot(decay_mat * scores, pseudo, precision=BEST_PRECISION)
    tail = jnp.where(doc_ids == doc_ids[-1], jnp.exp(cumulative[-1] - cumulative), 0.0)
    new_state = reach[-1] * state_mat + jnp.dot(key_vecs.T, tail[:, None] * pseudo, precision=BEST_PRECISION)
    return ((new_state, doc_ids[-1]), outputs)

def run_head(queries, key_vecs, value_vecs, beta_rate, log_decay, doc_ids, state_mat, prior_doc):
    tok_count = queries.shape[0]
    n_blocks = tok_count // STRETCH

    def split_blocks(member):
        return member.reshape((n_blocks, STRETCH) + member.shape[1:])
    pieces = tuple((split_blocks(member) for member in (queries, key_vecs, value_vecs, beta_rate, log_decay, doc_ids)))
    (final_state, last_doc), outputs = lax.scan(jax.checkpoint(stretch_step), (state_mat, prior_doc), pieces)
    return (final_state, outputs.reshape(tok_count, value_vecs.shape[-1]))

def gate_out(o_heads, gate_vals, gain_vec):
    tok_count = o_heads.shape[0]
    head_count = o_heads.shape[1]
    normed = rms_rows(o_heads, gain_vec) * jax.nn.silu(gate_vals.reshape(tok_count, head_count, DV))
    return normed.reshape(tok_count, head_count * DV)

def layer_forward(x_rows, params, doc_ids):
    attn_gain, w_query, w_key, w_value, w_gate, w_alpha, w_beta, conv_query, conv_key, conv_value, a_log, dt_bias, head_gain, w_out, mlp_gain, w_ffgate, w_ffup, w_down = params

    def hdot(left, right):
        return jnp.dot(left, right, precision=BEST_PRECISION)
    h_one = low(rms_rows(x_rows, attn_gain))
    q_pre = low(low_back(hdot(h_one, w_query)))
    k_pre = low(low_back(hdot(h_one, w_key)))
    v_pre = low(low_back(hdot(h_one, w_value)))
    gate_vals = low_back(hdot(h_one, w_gate))
    alpha_logit = low_back(hdot(h_one, w_alpha))
    beta_logit = low_back(hdot(h_one, w_beta))
    pad_rows = KCONV - 1
    doc_pad = jnp.concatenate([jnp.full((pad_rows,), -1, jnp.int32), doc_ids])
    q_pad = jnp.concatenate([jnp.zeros((pad_rows, q_pre.shape[1]), jnp.float32), q_pre])
    k_pad = jnp.concatenate([jnp.zeros((pad_rows, k_pre.shape[1]), jnp.float32), k_pre])
    v_pad = jnp.concatenate([jnp.zeros((pad_rows, v_pre.shape[1]), jnp.float32), v_pre])
    queries, key_vecs, value_vecs, beta_rate, log_decay = mixer_inputs(q_pad, k_pad, v_pad, alpha_logit, beta_logit, conv_query, conv_key, conv_value, a_log, dt_bias, doc_pad)
    start_state = jnp.zeros((H, DK, DV), jnp.float32)
    prior_doc = jnp.array(-1, jnp.int32)
    final_state, head_out = jax.vmap(run_head, in_axes=(0, 0, 0, 0, 0, None, 0, None))(jnp.swapaxes(queries, 0, 1), jnp.swapaxes(key_vecs, 0, 1), jnp.swapaxes(value_vecs, 0, 1), beta_rate.T, log_decay.T, doc_ids, start_state, prior_doc)
    o_heads = jnp.swapaxes(head_out, 0, 1)
    gated = low(gate_out(o_heads, gate_vals, head_gain))
    attn = low_back(hdot(gated, w_out))
    x_one = x_rows + attn
    h_two = low(rms_rows(x_one, mlp_gain))
    ff_gate = low_back(hdot(h_two, w_ffgate))
    ff_up = low_back(hdot(h_two, w_ffup))
    hidden = low(jax.nn.silu(ff_gate) * ff_up)
    mlp = low_back(hdot(hidden, w_down))
    return x_one + mlp

def reference(block_input, cotangent, doc_lengths, attn_gain, w_query, w_key, w_value, w_gate, w_alpha, w_beta, conv_query, conv_key, conv_value, a_log, dt_bias, head_gain, w_out, mlp_gain, w_ffgate, w_ffup, w_down):
    params = tuple((member.astype(jnp.float32) for member in (attn_gain, w_query, w_key, w_value, w_gate, w_alpha, w_beta, conv_query, conv_key, conv_value, a_log, dt_bias, head_gain, w_out, mlp_gain, w_ffgate, w_ffup, w_down)))
    seq_count = MB * BATCH
    x_all = block_input.reshape(seq_count, SEQ_LEN, D).astype(jnp.float32)
    cot_all = cotangent.reshape(seq_count, SEQ_LEN, D).astype(jnp.float32)
    len_all = doc_lengths.reshape(seq_count, NDOC)

    def one_sequence(running, member):
        x_rows, cot_rows, lengths = member
        doc_ends = jnp.cumsum(lengths).astype(jnp.int32)
        positions = jnp.arange(SEQ_LEN, dtype=jnp.int32)
        doc_ids = lax.optimization_barrier(jnp.sum((positions[:, None] >= doc_ends[None, :]).astype(jnp.int32), axis=1)).astype(jnp.int32)
        out_rows, back_fn = jax.vjp(lambda rows_in, params_in: layer_forward(rows_in, params_in, doc_ids), x_rows, params)
        dx_rows, d_params = back_fn(cot_rows)
        running = jax.tree.map(lambda acc, new: acc + new, running, d_params)
        return (running, (out_rows, dx_rows))
    zero_grads = jax.tree.map(jnp.zeros_like, params)
    grads, (y_all, dx_all) = lax.scan(one_sequence, zero_grads, (x_all, cot_all, len_all))
    block_output = y_all.reshape(MB, BATCH, SEQ_LEN, D).astype(jnp.bfloat16)
    input_grad = dx_all.reshape(MB, BATCH, SEQ_LEN, D)
    g_attn_gain, g_query, g_key, g_value, g_gate, g_alpha, g_beta, g_conv_q, g_conv_k, g_conv_v, g_alog, g_bias, g_head_gain, g_out, g_mlp_gain, g_ffgate, g_ffup, g_down = grads
    return (block_output, input_grad, g_query, g_key, g_value, g_gate, g_alpha, g_beta, g_out, g_ffgate, g_ffup, g_down, g_attn_gain, g_mlp_gain, g_head_gain, g_conv_q, g_conv_k, g_conv_v, g_alog, g_bias)
```

```python
import math

import jax
import jax.numpy as jnp
from jax import lax
from jax.experimental import pallas as pl
from jax.experimental.pallas import tpu as pltpu
from jax.sharding import PartitionSpec as P

DK = 128
DV = 256
KCONV = 4
CHUNK = 128
PAD = 16
LANES = 128
FAR = -(1 << 20)
VMEM_BYTES = 56 * 1024 * 1024

F32 = jnp.float32
BF16 = jnp.bfloat16
BEST = lax.Precision.HIGHEST
SEQ_FSDP = ("seq", "fsdp")


def dot(left, right, left_dim=1, right_dim=0):
    return lax.dot_general(
        left, right, (((left_dim,), (right_dim,)), ((), ())), preferred_element_type=F32
    )


def split_two(value):
    high = value.astype(BF16)
    return high, (value - high.astype(F32)).astype(BF16)


def sigmoid(value):
    return 1.0 / (1.0 + jnp.exp(-value))


def rounded(value):
    return value.astype(BF16).astype(F32)


def row_sum(value):
    return jnp.sum(value, axis=1, keepdims=True)


def twice(value):
    return jnp.concatenate([value, value], axis=1)


def taps_of(padded, since_start):
    taps = [padded[PAD:]]
    for shift in range(1, KCONV):
        moved = pltpu.roll(padded, shift, 0)[PAD:]
        taps.append(jnp.where(since_start >= shift, moved, 0.0))
    return taps


def filtered(taps, filters):
    total = taps[0] * filters[KCONV - 1 : KCONV]
    for shift in range(1, KCONV):
        total = total + taps[shift] * filters[KCONV - 1 - shift : KCONV - shift]
    return total


def unfiltered(grads, filters, since_start):
    zero_rows = jnp.zeros((PAD, grads.shape[1]), F32)
    total = jnp.concatenate([zero_rows, grads * filters[KCONV - 1 : KCONV]], axis=0)
    rows = total.shape[0]
    for shift in range(1, KCONV):
        part = jnp.where(since_start >= shift, grads, 0.0)
        part = part * filters[KCONV - 1 - shift : KCONV - shift]
        part = jnp.concatenate([zero_rows, part], axis=0)
        total = total + pltpu.roll(part, rows - shift, 0)
    return total


def row_of(table, row):
    rows = lax.broadcasted_iota(jnp.int32, table.shape, 0)
    return jnp.sum(jnp.where(rows == row, table, 0.0), axis=0, keepdims=True)


def softplus(value):
    return jnp.maximum(value, 0.0) + jnp.log(1.0 + jnp.exp(-jnp.abs(value)))


def three_parts(value):
    high = value.astype(BF16).astype(F32)
    middle = (value - high).astype(BF16).astype(F32)
    return high, middle, value - high - middle


def stack_rows(rows):
    height = -(-len(rows) // 16) * 16
    place = lax.broadcasted_iota(jnp.int32, (height, rows[0].shape[1]), 0)
    out = jnp.zeros((height, rows[0].shape[1]), F32)
    for at, row in enumerate(rows):
        out = jnp.where(place == at, row, out)
    return out.astype(BF16)


def spread(rows):
    parts = [part for row in rows for part in three_parts(row)]
    stacked = stack_rows(parts)
    shape = (stacked.shape[0], LANES * len(rows))
    place = lax.broadcasted_iota(jnp.int32, shape, 0)
    lane = lax.broadcasted_iota(jnp.int32, shape, 1)
    mine = (place >= (lane // LANES) * 3) & (place < (lane // LANES) * 3 + 3)
    wide = dot(stacked, jnp.where(mine, 1.0, 0.0).astype(BF16), 0, 0)
    return [wide[:, at * LANES : (at + 1) * LANES] for at in range(len(rows))]


def squares_iota():
    rows = lax.broadcasted_iota(jnp.int32, (CHUNK, CHUNK), 0)
    cols = lax.broadcasted_iota(jnp.int32, (CHUNK, CHUNK), 1)
    return rows, cols


def token_rows(ends_ref, logits_ref, params_ref, micro, head, heads, first):
    table = logits_ref[PAD + first : PAD + first + CHUNK, :].T[:8]
    params = params_ref[...]
    lanes = lax.broadcasted_iota(jnp.int32, params.shape, 1)
    params = row_sum(jnp.where(lanes == head, params, 0.0))
    scale = jnp.exp(params[0:1])
    argument = row_of(table, head) + params[1:2]
    beta = sigmoid(row_of(table, heads + head))
    log_decay = -scale * softplus(argument)
    slope = -scale * sigmoid(argument)
    rows, cols = squares_iota()
    upto = jnp.where(rows <= cols, 1.0, 0.0).astype(BF16)
    run = jnp.sum(dot(stack_rows(three_parts(log_decay)), upto), axis=0, keepdims=True)
    position = first + lax.broadcasted_iota(jnp.int32, (1, CHUNK), 1)
    start = jnp.full((1, CHUNK), FAR, jnp.int32)
    for at in range(ends_ref.shape[1]):
        edge = ends_ref[micro, at]
        start = jnp.where(position >= edge, edge, start)
    return beta, log_decay, slope, run, start.astype(F32)


def inverse_unit_lower(stricts):
    rows, cols = squares_iota()
    eye = jnp.where(rows == cols, 1.0, 0.0)

    def corner(width):
        inside = (rows // (2 * width)) == (cols // (2 * width))
        return inside & (rows % (2 * width) >= width) & (cols % (2 * width) < width)

    inverses = [eye - jnp.where(corner(1), strict, 0.0) for strict in stricts]
    width = 2
    while width < CHUNK:
        mask = corner(width)
        held = [inverse.astype(BF16) for inverse in inverses]
        edges = [jnp.where(mask, strict, 0.0).astype(BF16) for strict in stricts]
        lefts = [dot(one, edge).astype(BF16) for one, edge in zip(held, edges)]
        steps = [dot(left, one) for left, one in zip(lefts, held)]
        inverses = [inverse - step for inverse, step in zip(inverses, steps)]
        width *= 2
    out = []
    for strict, inverse in zip(stricts, inverses):
        strict_hi, strict_lo = split_two(strict)
        inv_hi, inv_lo = split_two(inverse)
        product = dot(strict_hi, inv_hi) + dot(strict_hi, inv_lo) + dot(strict_lo, inv_hi)
        out.append((inverse, (eye - inverse - product).astype(BF16), inv_hi))
    return [inverse + dot(inv_hi, miss) for inverse, miss, inv_hi in out]


def decay_terms(run_rows, run_cols, start, first):
    rows, cols = squares_iota()
    allowed = (cols <= rows) & ((cols + first).astype(F32) >= start)
    within = jnp.where(allowed, jnp.exp(jnp.minimum(run_rows - run_cols, 0.0)), 0.0)
    strict = jnp.where(cols < rows, within, 0.0)
    reach = jnp.where(start < first, jnp.exp(run_rows), 0.0)
    last = run_rows[CHUNK - 1 :]
    last_start = start[CHUNK - 1 :]
    tail = jnp.where((rows + first).astype(F32) >= last_start, jnp.exp(last - run_rows), 0.0)
    return within, strict, reach, tail, reach[CHUNK - 1 :]


def ages(starts):
    start = jnp.concatenate(starts, axis=0)
    return lax.broadcasted_iota(jnp.int32, start.shape, 0).astype(F32) - start


def normalized(conved):
    gate = sigmoid(conved)
    active = conved * gate
    inv = lax.rsqrt(row_sum(active * active) + 1e-06)
    return active * inv, inv, gate


def local_kernel(heads, with_trans):
    def body(
        ends_ref, q_ref, k_ref, v_ref, logits_ref, fq_ref, fk_ref, fv_ref, params_ref, *outs
    ):
        qe_ref, ol_ref, mt_ref, nn_ref, ti_ref, rl_ref, rr_ref, fin_ref = outs[:8]
        micro, head = pl.program_id(0), pl.program_id(1)
        rows = q_ref.shape[0] - PAD
        chunks = range(rows // CHUNK)
        parts = [slice(c * CHUNK, (c + 1) * CHUNK) for c in chunks]
        found = [
            token_rows(ends_ref, logits_ref, params_ref, micro, head, heads, c * CHUNK)
            for c in chunks
        ]
        for c in chunks:
            for at, row in enumerate(found[c]):
                rr_ref[at : at + 1, parts[c]] = row
        spreads = [spread([run, beta, start]) for beta, _, _, run, start in found]
        since = ages([one[2] for one in spreads])
        since_wide = twice(since)
        decays = [
            decay_terms(spreads[c][0], found[c][3], spreads[c][2], c * CHUNK) for c in chunks
        ]
        k_conv = filtered(taps_of(rounded(k_ref[...]), since), fk_ref[...])
        keys = normalized(k_conv)[0]
        keys_b = keys.astype(BF16)
        betas = [one[1] for one in spreads]
        grams = [dot(keys_b[part], keys_b[part], 1, 1) for part in parts]
        inverses = inverse_unit_lower(
            [b * decay[1] * gram for b, decay, gram in zip(betas, decays, grams)]
        )
        q_conv = filtered(taps_of(rounded(q_ref[...]), since), fq_ref[...])
        v_conv = filtered(taps_of(rounded(v_ref[...]), since_wide), fv_ref[...])
        queries = normalized(q_conv)[0] * (1.0 / math.sqrt(DK))
        queries_b = queries.astype(BF16)
        values = v_conv * sigmoid(v_conv)
        scores = [dot(queries_b[part], keys_b[part], 1, 1) for part in parts]
        solved = []
        for c, part in zip(chunks, parts):
            within, strict, reach, tail, through = decays[c]
            sides = jnp.concatenate(
                [betas[c] * reach * keys[part], twice(betas[c]) * values[part]], axis=1
            )
            inv_b = inverses[c].astype(BF16)
            ti_ref[part, :] = inv_b
            solved.append(dot(inv_b, sides.astype(BF16)).astype(BF16))
        shifts, adds = [], []
        for c, part in zip(chunks, parts):
            within, strict, reach, tail, through = decays[c]
            out_part = dot((within * scores[c]).astype(BF16), solved[c])
            state_part = dot((tail * keys[part]).astype(BF16), solved[c], 0, 0)
            qe_ref[part, :] = (reach * queries[part] - out_part[:, :DK]).astype(BF16)
            ol_ref[part, :] = out_part[:, DK:]
            shifts.append(state_part[:, :DK].astype(BF16))
            adds.append(state_part[:, DK:])
            mt_ref[part, :] = shifts[c]
            nn_ref[part, :] = adds[c]
            rl_ref[c : c + 1, :] = through
        state = adds[0]
        for c in chunks[1:]:
            moved = dot(shifts[c], state.astype(BF16))
            state = twice(decays[c][4]) * state - moved + adds[c]
        fin_ref[...] = state.astype(fin_ref.dtype)
        if with_trans:
            square_rows, square_cols = squares_iota()
            trans = jnp.where(square_rows == square_cols, 1.0, 0.0)
            for c in chunks:
                trans = decays[c][4] * trans - dot(shifts[c], trans.astype(BF16))
            outs[8][...] = trans

    return body


def slot_of(slots_ref, chunk, per_block):
    first = slots_ref[chunk // per_block] * per_block + chunk % per_block
    return pl.ds(pl.multiple_of(first * CHUNK, CHUNK), CHUNK)


def output_kernel(per_block):
    def body(
        slots_ref,
        inc_ref,
        qe_ref,
        ol_ref,
        mt_ref,
        nn_ref,
        rl_ref,
        gate_ref,
        gain_ref,
        wo_ref,
        og_ref,
        o_ref,
        st_ref,
        keep_ref,
        give_ref,
        sum_scr,
    ):
        rows = qe_ref.shape[0]
        head = pl.program_id(0)
        state = inc_ref[...].astype(F32)
        gain = gain_ref[0:1, :]
        for chunk in range(rows // CHUNK):
            first = chunk * CHUNK
            part = slice(first, first + CHUNK)
            state_b = state.astype(BF16)
            st_ref[part, :] = state_b
            pair = jnp.concatenate([qe_ref[part, :], mt_ref[part, :]], axis=0)
            both = dot(pair, state_b)
            out = both[:CHUNK] + ol_ref[part, :]
            o_ref[part, :] = out
            gate = gate_ref[PAD + first : PAD + first + CHUNK, :].astype(F32)
            norm = lax.rsqrt(jnp.mean(out * out, axis=1, keepdims=True) + 1e-05)
            gated = (out * norm * gain * (gate * sigmoid(gate))).astype(BF16)
            og_ref[slot_of(slots_ref, chunk, per_block), :] = gated
            through = twice(rl_ref[chunk : chunk + 1, :])
            state = through * state - both[CHUNK:] + nn_ref[part, :]
        product = dot(og_ref[...], wo_ref[...], 1, 1)

        @pl.when(head == 0)
        def _():
            sum_scr[...] = product

        @pl.when(head > 0)
        def _():
            sum_scr[...] += product

        @pl.when(head == pl.num_programs(0) - 1)
        def _():
            half = rows // 2
            keep_ref[...] = sum_scr[:half, :].astype(BF16)
            give_ref[...] = sum_scr[half:, :].astype(BF16)

    return body


def gate_back_kernel(per_block):
    def body(
        slots_ref,
        low_ref,
        high_ref,
        o_ref,
        gate_ref,
        gain_ref,
        qe_ref,
        mt_ref,
        rl_ref,
        wo_ref,
        do_ref,
        hg_ref,
        dgate_ref,
        dattn_ref,
        gf_ref,
        gg_ref,
        dog_scr,
    ):
        rows = qe_ref.shape[0]
        gain = gain_ref[0:1, :]
        grad_gain = jnp.zeros((1, DV), F32)
        dgate_ref[:PAD, :] = jnp.zeros((PAD, DV), BF16)
        half = rows // 2
        dog_scr[:half, :] = dot(low_ref[...], wo_ref[...])
        dog_scr[half:, :] = dot(high_ref[...], wo_ref[...])
        state = None
        for chunk in reversed(range(rows // CHUNK)):
            first = chunk * CHUNK
            part = slice(first, first + CHUNK)
            out = o_ref[part, :]
            gate = gate_ref[PAD + first : PAD + first + CHUNK, :].astype(F32)
            dog = dog_scr[slot_of(slots_ref, chunk, per_block), :]
            norm = lax.rsqrt(jnp.mean(out * out, axis=1, keepdims=True) + 1e-05)
            unit = out * norm
            sig = sigmoid(gate)
            swish = gate * sig
            grad_gain = grad_gain + jnp.sum(dog * unit * swish, axis=0, keepdims=True)
            d_gate = dog * unit * gain * (sig * (1.0 + gate * (1.0 - sig)))
            dgate_ref[PAD + first : PAD + first + CHUNK, :] = d_gate.astype(BF16)
            d_unit = dog * gain * swish
            d_out = norm * (d_unit - unit * jnp.mean(d_unit * unit, axis=1, keepdims=True))
            d_out_b = d_out.astype(BF16)
            do_ref[part, :] = d_out_b
            added = dot(qe_ref[part, :], d_out_b, 0, 0)
            hg_ref[part, :] = added
            if state is None:
                state = added
            else:
                moved = dot(mt_ref[part, :], state.astype(BF16), 0, 0)
                state = twice(rl_ref[chunk : chunk + 1, :]) * state - moved + added
        gf_ref[...] = state.astype(gf_ref.dtype)
        first_head = pl.program_id(0) == 0

        @pl.when(first_head)
        def _():
            dattn_ref[:half, :] = low_ref[...]
            dattn_ref[half:, :] = high_ref[...]
            gg_ref[...] = jnp.broadcast_to(grad_gain, gg_ref.shape)

        @pl.when(jnp.logical_not(first_head))
        def _():
            gg_ref[...] += jnp.broadcast_to(grad_gain, gg_ref.shape)

    return body


def feed_forward_kernel(
    low_ref, high_ref, cot_ref, w_ref, keep_ref, give_ref, h_ref, hid_ref, dg_ref, du_ref
):
    shards, shard = w_ref.shape[0], w_ref.shape[3]
    half = low_ref.shape[0]
    width = shards * shard
    h_ref[:half, :] = low_ref[...]
    h_ref[half:, :] = high_ref[...]

    def spans(at):
        return slice(at * shard, (at + 1) * shard)

    def entering(ref, which):
        total = None
        for at in range(shards):
            part = dot(ref[:, spans(at)], w_ref[at, which], 1, 1)
            total = part if total is None else total + part
        return total

    gate = entering(h_ref, 0)
    sig = sigmoid(gate)
    swish = gate * sig
    up = entering(h_ref, 1)
    hidden = (swish * up).astype(BF16)
    hid_ref[...] = hidden
    d_hidden = entering(cot_ref, 2)
    d_gate = (d_hidden * up * sig * (1.0 + gate * (1.0 - sig))).astype(BF16)
    d_up = (d_hidden * swish).astype(BF16)
    dg_ref[...] = d_gate
    du_ref[...] = d_up
    for at in range(shards):
        out = dot(hidden, w_ref[at, 2]).astype(BF16)
        d_h = (dot(d_gate, w_ref[at, 0]) + dot(d_up, w_ref[at, 1])).astype(BF16)
        shifted = slice(width + at * shard, width + (at + 1) * shard)
        keep_ref[:, spans(at)] = out[:half]
        give_ref[:, spans(at)] = out[half:]
        keep_ref[:, shifted] = d_h[:half]
        give_ref[:, shifted] = d_h[half:]


def back_kernel(heads):
    def body(
        q_ref,
        k_ref,
        v_ref,
        rr_ref,
        fq_ref,
        fk_ref,
        fv_ref,
        ti_ref,
        st_ref,
        mt_ref,
        rl_ref,
        hg_ref,
        gin_ref,
        do_ref,
        dext_ref,
        own_ref,
        small_ref,
        dq_scr,
        dk_scr,
        dv_scr,
    ):
        head = pl.program_id(0)
        rows = q_ref.shape[0] - PAD
        logits_at = dext_ref.shape[1] - LANES
        chunks = range(rows // CHUNK)
        parts = [slice(c * CHUNK, (c + 1) * CHUNK) for c in chunks]

        @pl.when(head == 0)
        def _():
            dext_ref[...] = jnp.zeros(dext_ref.shape, BF16)
            small_ref[...] = jnp.zeros(small_ref.shape, F32)

        grads = [None for _ in chunks]
        grad_state = gin_ref[...].astype(F32)
        for c in reversed(chunks):
            grads[c] = grad_state.astype(BF16)
            if c:
                moved = dot(mt_ref[parts[c], :], grads[c], 0, 0)
                through = twice(rl_ref[c : c + 1, :])
                grad_state = through * grad_state - moved + hg_ref[parts[c], :]
        found = [[rr_ref[at : at + 1, part] for at in range(5)] for part in parts]
        spreads = [
            spread([run, beta, start, log_decay, slope])
            for beta, log_decay, slope, run, start in found
        ]
        since = ages([one[2] for one in spreads])
        since_wide = twice(since)
        decays = [
            decay_terms(spreads[c][0], found[c][3], spreads[c][2], c * CHUNK) for c in chunks
        ]
        fq, fk, fv = fq_ref[...], fk_ref[...], fv_ref[...]
        q_taps = taps_of(rounded(q_ref[...]), since)
        k_taps = taps_of(rounded(k_ref[...]), since)
        v_taps = taps_of(rounded(v_ref[...]), since_wide)
        q_conv, k_conv, v_conv = filtered(q_taps, fq), filtered(k_taps, fk), filtered(v_taps, fv)
        q_unit, q_inv, q_gate = normalized(q_conv)
        keys, k_inv, k_gate = normalized(k_conv)
        q_scale = 1.0 / math.sqrt(DK)
        queries = q_unit * q_scale
        v_gate = sigmoid(v_conv)
        values = v_conv * v_gate
        keys_b, queries_b = keys.astype(BF16), queries.astype(BF16)
        square_rows, square_cols = squares_iota()
        later = jnp.where(square_cols >= square_rows, 1.0, 0.0).astype(BF16)
        lanes = lax.broadcasted_iota(jnp.int32, (CHUNK, LANES), 1)
        sums = [jnp.zeros((1, 1), F32), jnp.zeros((1, 1), F32)]
        for c in reversed(chunks):
            part = parts[c]
            within, strict, reach, tail, through = decays[c]
            run, b, start, log_decay, slope = spreads[c]
            k, q, v = keys[part], queries[part], values[part]
            k_b, q_b = keys_b[part], queries_b[part]
            inv_b = ti_ref[part, :]
            state_b = st_ref[part, :]
            grad_b = grads[c]
            d_out = do_ref[part, :]
            gram = dot(k_b, k_b, 1, 1)
            raw = dot(q_b, k_b, 1, 1)
            scores_b = (within * raw).astype(BF16)
            from_both = dot(k_b, jnp.concatenate([state_b, grad_b], axis=1))
            side = twice(b) * (v - twice(reach) * from_both[:, :DV])
            pseudo_b = dot(inv_b, side.astype(BF16)).astype(BF16)
            d_pseudo = dot(scores_b, d_out, 0, 0) + twice(tail) * from_both[:, DV:]
            d_side = dot(inv_b, d_pseudo.astype(BF16), 0, 0)
            d_side_b = d_side.astype(BF16)
            out_and_side = jnp.concatenate([d_out, d_side_b], axis=0)
            squares = dot(out_and_side, pseudo_b, 1, 1)
            by_state = dot(out_and_side, state_b, 1, 1)
            by_grad = dot(pseudo_b, grad_b, 1, 1)
            out_state, side_state = by_state[:CHUNK], by_state[CHUNK:]
            d_raw = within * squares[:CHUNK]
            solve_grad = squares[CHUNK:] * strict
            d_gram = -(b * solve_grad)
            d_raw_b, d_gram_b = d_raw.astype(BF16), d_gram.astype(BF16)
            d_q = reach * out_state + dot(d_raw_b, k_b)
            d_k = tail * by_grad - b * reach * side_state
            d_k = d_k + dot(d_raw_b, q_b, 0, 0) + dot(d_gram_b, k_b) + dot(d_gram_b, k_b, 0, 0)
            dv_scr[part, :] = twice(b) * d_side
            dq_scr[part, :] = d_q
            dk_scr[part, :] = d_k
            side_key = row_sum(k * side_state)
            d_beta = row_sum(d_side * v) - row_sum(solve_grad * gram) - reach * side_key
            weight = d_raw * raw + d_gram * gram
            reach_part = reach * (row_sum(q * out_state) - b * side_key)
            tail_part = tail * row_sum(k * by_grad)
            d_run = row_sum(weight - weight.T) + reach_part - tail_part
            kept = jnp.sum(grad_b.astype(F32) * state_b.astype(F32), axis=0, keepdims=True)
            kept = through * row_sum(kept)
            end_grad = jnp.sum(tail_part, axis=0, keepdims=True) + kept
            run_hi, run_lo = split_two(d_run)
            d_decay = dot(later, run_hi) + dot(later, run_lo) + end_grad
            d_alpha = d_decay * slope
            d_beta_logit = d_beta * b * (1.0 - b)
            sums[0] = sums[0] + jnp.sum((d_decay * log_decay)[:, :1], axis=0, keepdims=True)
            sums[1] = sums[1] + jnp.sum(d_alpha[:, :1], axis=0, keepdims=True)
            place = slice(PAD + c * CHUNK, PAD + (c + 1) * CHUNK)
            held = dext_ref[place, logits_at:].astype(F32)
            held = jnp.where(lanes == head, d_alpha, held)
            held = jnp.where(lanes == heads + head, d_beta_logit, held)
            dext_ref[place, logits_at:] = held.astype(BF16)

        def channel_back(d_conv, taps, filters, since_here, at, width):
            place = pl.ds(pl.multiple_of(at, LANES), width)
            dext_ref[:, place] = unfiltered(d_conv, filters, since_here).astype(BF16)
            for shift in range(KCONV):
                grad = jnp.sum(d_conv * taps[shift], axis=0, keepdims=True)
                small_ref[KCONV - 1 - shift : KCONV - shift, place] = grad

        def unit_back(d_unit, unit, inv, conv, gate):
            d_active = inv * (d_unit - unit * row_sum(d_unit * unit))
            return d_active * gate * (1.0 + conv * (1.0 - gate))

        d_q_conv = unit_back(dq_scr[...] * q_scale, q_unit, q_inv, q_conv, q_gate)
        d_k_conv = unit_back(dk_scr[...], keys, k_inv, k_conv, k_gate)
        d_v_conv = dv_scr[...] * v_gate * (1.0 + v_conv * (1.0 - v_gate))
        channel_back(d_q_conv, q_taps, fq, since, head * DK, DK)
        channel_back(d_k_conv, k_taps, fk, since, (heads + head) * DK, DK)
        channel_back(d_v_conv, v_taps, fv, since_wide, 2 * heads * DK + head * DV, DV)
        rate_rows = lax.broadcasted_iota(jnp.int32, (8, LANES), 0)
        rate_lanes = lax.broadcasted_iota(jnp.int32, (8, LANES), 1)
        rates = jnp.where(rate_rows == 0, sums[0], jnp.where(rate_rows == 1, sums[1], 0.0))
        small_ref[:, logits_at:] += jnp.where(rate_lanes == head, rates, 0.0)

        @pl.when(head == pl.num_programs(0) - 1)
        def _():
            own_ref[...] = dext_ref[...]

    return body


def whole(shape):
    return pl.BlockSpec((None,) + shape, lambda m, h, *_: (m, 0, 0))


def per_head(shape):
    return pl.BlockSpec((None, None) + shape, lambda m, h, *_: (m, h, 0, 0))


def columns(rows, width, skip=0):
    return pl.BlockSpec((None, rows, width), lambda m, h, *_: (m, 0, skip + h))


def filter_cols(width):
    return pl.BlockSpec((KCONV, width), lambda m, h, *_: (0, h))


def fixed(shape):
    return pl.BlockSpec(shape, lambda m, h, *_: (0, 0))


def kernel_params(axes=2):
    return pltpu.CompilerParams(
        dimension_semantics=("arbitrary",) * axes, vmem_limit_bytes=VMEM_BYTES
    )


def busy(microseconds):
    return pl.CostEstimate(
        flops=0, transcendentals=0, bytes_accessed=int(microseconds * 3.3e6)
    )


class Shared:
    def __init__(self, micros):
        self.micros = micros
        self.arrays = None

    def call(self, body, micro, grid, prefetch, operands, in_specs, out, scratch, name, cost):
        shared = [at for at, one in enumerate(out) if one[4]]
        held = [] if self.arrays is None else self.arrays
        skip = len(prefetch) + len(operands)

        def wrapped(*refs):
            body(*refs[:skip], *refs[skip + len(held) :])

        out_shape, out_specs = [], []
        for shape, dtype, block, index, is_shared in out:
            leading = (self.micros,) if is_shared else (1,)
            first = micro if is_shared else 0
            out_shape.append(jax.ShapeDtypeStruct(leading + shape, dtype))
            out_specs.append(
                pl.BlockSpec((None,) + block, lambda *g, i=index, f=first: (f,) + i(*g))
            )
        results = pl.pallas_call(
            wrapped,
            grid_spec=pltpu.PrefetchScalarGridSpec(
                num_scalar_prefetch=len(prefetch),
                grid=grid,
                in_specs=in_specs + [pl.BlockSpec(memory_space=pl.ANY)] * len(held),
                out_specs=out_specs,
                scratch_shapes=scratch,
            ),
            out_shape=out_shape,
            input_output_aliases={skip + at: shared[at] for at in range(len(held))},
            compiler_params=kernel_params(len(grid)),
            cost_estimate=busy(cost),
            name=name,
        )(*prefetch, *operands, *held)
        self.arrays = [results[at] for at in shared]
        return [one for at, one in enumerate(results) if at not in shared]


def by_head(h, *_):
    return (h, 0, 0)


def by_column(h, *_):
    return (0, h)


def at_origin(*_):
    return (0, 0)


def mixer_specs(heads, padded):
    return [
        columns(padded, DK),
        columns(padded, DK, heads),
        columns(padded, DV, heads * DK * 2 // DV),
    ]


def filter_specs():
    return [filter_cols(DK), filter_cols(DK), filter_cols(DV)]


def run_local(ends, pre, filters, params, heads, with_trans):
    micros, padded = pre.shape[0], pre.shape[1]
    rows = padded - PAD
    logits_at = pre.shape[2] // LANES - 1
    shapes = [
        ((rows, DK), BF16),
        ((rows, heads * DV), F32),
        ((rows, DK), BF16),
        ((rows, DV), F32),
        ((rows, CHUNK), BF16),
        ((8, LANES), F32),
        ((8, rows), F32),
        ((DK, DV), BF16),
    ]
    if with_trans:
        shapes.append(((DK, DK), F32))
    out_shape, out_specs = [], []
    for at, (shape, dtype) in enumerate(shapes):
        if at == 1:
            out_shape.append(jax.ShapeDtypeStruct((micros,) + shape, dtype))
            out_specs.append(columns(rows, DV))
        else:
            out_shape.append(jax.ShapeDtypeStruct((micros, heads) + shape, dtype))
            out_specs.append(per_head(shape))
    logits_spec = pl.BlockSpec((None, padded, LANES), lambda m, h, *_: (m, 0, logits_at))
    return pl.pallas_call(
        local_kernel(heads, with_trans),
        grid_spec=pltpu.PrefetchScalarGridSpec(
            num_scalar_prefetch=1,
            grid=(micros, heads),
            in_specs=mixer_specs(heads, padded)
            + [logits_spec]
            + filter_specs()
            + [fixed((8, LANES))],
            out_specs=out_specs,
        ),
        out_shape=out_shape,
        compiler_params=kernel_params(),
        cost_estimate=busy(10.0 * micros),
        name="mixer_local",
    )(ends, pre, pre, pre, pre, *filters, params)


def one_head(shape):
    return pl.BlockSpec((None, None) + shape, lambda h, *_: (0, h, 0, 0))


def one_column(rows, width, skip=0):
    return pl.BlockSpec((None, rows, width), lambda h, *_: (0, 0, skip + h))


def one_whole(shape, micro=0):
    return pl.BlockSpec((None,) + shape, lambda *_: (micro,) + (0,) * len(shape))


def gain_spec():
    return pl.BlockSpec((8, DV), at_origin)


def run_output(shared, micro, slots, incoming, saved, gate, gain, w_out):
    qe, ol, mt, nn, ti, rl, rr = saved
    heads, rows = qe.shape[1:3]
    width = w_out.shape[0]
    half = (rows // 2, width)
    return shared.call(
        output_kernel(rows // slots.shape[0] // CHUNK),
        micro,
        (heads,),
        [slots],
        [incoming, qe, ol, mt, nn, rl, gate, gain, w_out],
        [
            one_head((DK, DV)),
            one_head((rows, DK)),
            one_column(rows, DV),
            one_head((rows, DK)),
            one_head((rows, DV)),
            one_head((8, LANES)),
            one_column(rows + PAD, DV),
            gain_spec(),
            pl.BlockSpec((width, DV), lambda h, *_: (0, heads + h)),
        ],
        [
            ((rows, heads * DV), BF16, (rows, DV), by_column, True),
            ((rows, heads * DV), F32, (rows, DV), by_column, False),
            ((heads, rows, DV), BF16, (None, rows, DV), by_head, False),
            (half, BF16, half, at_origin, False),
            (half, BF16, half, at_origin, False),
        ],
        [pltpu.VMEM((rows, width), F32)],
        "mixer_output",
        6.0,
    )


def run_gate_back(shared, micro, slots, d_attn, out, gate, gain, saved, w_out):
    qe, ol, mt, nn, ti, rl, rr = saved
    heads, rows = qe.shape[1:3]
    width = w_out.shape[0]
    return shared.call(
        gate_back_kernel(rows // slots.shape[0] // CHUNK),
        micro,
        (heads,),
        [slots],
        [*d_attn, out, gate, gain, qe, mt, rl, w_out],
        [one_whole((rows // 2, width))] * 2
        + [
            one_column(rows, DV),
            one_column(rows + PAD, DV),
            gain_spec(),
            one_head((rows, DK)),
            one_head((rows, DK)),
            one_head((8, LANES)),
            pl.BlockSpec((width, DV), lambda h, *_: (0, heads + h)),
        ],
        [
            ((rows, heads * DV), BF16, (rows, DV), by_column, False),
            ((heads, rows, DV), F32, (None, rows, DV), by_head, False),
            ((rows + PAD, heads * DV), BF16, (rows + PAD, DV), by_column, True),
            ((rows, width), BF16, (rows, width), at_origin, True),
            ((heads, DK, DV), BF16, (None, DK, DV), by_head, False),
            ((8, DV), F32, (8, DV), at_origin, False),
        ],
        [pltpu.VMEM((rows, DV), F32)],
        "mixer_gate_back",
        6.0,
    )


def run_feed_forward(shared, micro, h_two, cot, weights):
    rows, width = cot.shape[1:]
    hidden = weights.shape[2]
    sums = (rows // 2, 2 * width)
    kept = (rows, hidden)
    return shared.call(
        feed_forward_kernel,
        micro,
        (1,),
        [],
        [*h_two, cot, weights],
        [one_whole((rows // 2, width))] * 2
        + [
            one_whole((rows, width), micro),
            pl.BlockSpec(weights.shape, lambda *_: (0, 0, 0, 0)),
        ],
        [
            (sums, BF16, sums, at_origin, False),
            (sums, BF16, sums, at_origin, False),
            ((rows, width), BF16, (rows, width), at_origin, True),
            (kept, BF16, kept, at_origin, True),
            (kept, BF16, kept, at_origin, True),
            (kept, BF16, kept, at_origin, True),
        ],
        [],
        "feed_forward",
        9.0,
    )


def run_back(shared, micro, pre, filters, saved, states, added, incoming, d_out):
    qe, ol, mt, nn, ti, rl, rr = saved
    heads, rows = qe.shape[1:3]
    padded = rows + PAD
    width = pre.shape[2]
    return shared.call(
        back_kernel(heads),
        micro,
        (heads,),
        [],
        [pre, pre, pre, rr, *filters, ti, states, mt, rl, added, incoming, d_out],
        [
            one_column(padded, DK),
            one_column(padded, DK, heads),
            one_column(padded, DV, heads * DK * 2 // DV),
            one_head((8, rows)),
            pl.BlockSpec((KCONV, DK), by_column),
            pl.BlockSpec((KCONV, DK), by_column),
            pl.BlockSpec((KCONV, DV), by_column),
            one_head((rows, CHUNK)),
            one_head((rows, DV)),
            one_head((rows, DK)),
            one_head((8, LANES)),
            one_head((rows, DV)),
            one_head((DK, DV)),
            one_column(rows, DV),
        ],
        [
            ((padded, width), BF16, (padded, width), at_origin, True),
            ((padded, width), BF16, (padded, width), at_origin, False),
            ((8, width), F32, (8, width), at_origin, False),
        ],
        [
            pltpu.VMEM((rows, DK), F32),
            pltpu.VMEM((rows, DK), F32),
            pltpu.VMEM((rows, DV), F32),
        ],
        "mixer_back",
        14.0,
    )


def passed_along(block, axis, distance):
    devices = range(lax.axis_size(axis))
    route = [(i - distance, i) for i in devices if i - distance in devices]
    return lax.ppermute(block, axis, route)


def swapped(block, axis, bit):
    return lax.ppermute(block, axis, [(i, i ^ bit) for i in range(lax.axis_size(axis))])


def reversed_bits(value, size):
    out, bit = 0, 1
    while bit < size:
        out = out * 2 + (value // bit) % 2
        bit *= 2
    return out


def to_slots(rows, axis):
    place = lax.axis_index(axis)
    size = lax.axis_size(axis)
    count = rows.shape[1] // size
    owners = [place ^ reversed_bits(slot, size) for slot in range(size)]
    return jnp.concatenate(
        [lax.dynamic_slice_in_dim(rows, owner * count, count, 1) for owner in owners], axis=1
    )


def slot_table(axis):
    size = lax.axis_size(axis)
    away = jnp.arange(size, dtype=jnp.int32) ^ lax.axis_index(axis)
    return reversed_bits(away, size).astype(jnp.int32)


class Scatter:
    def __init__(self, keep, give, axis):
        self.axis, self.bit, self.keep = axis, 1, keep.astype(F32)
        self.send(give)

    def send(self, give):
        self.sent = give.astype(BF16)
        self.got = swapped(self.sent, self.axis, self.bit)

    def advance(self, *waits):
        parts = self.keep + after(self.got, *waits).astype(F32)
        self.bit *= 2
        if self.bit >= lax.axis_size(self.axis):
            return parts
        half = parts.shape[1] // 2
        self.keep = parts[:, :half]
        self.send(parts[:, half:])
        return None

    def finish(self, *waits):
        result = None
        while result is None:
            result = self.advance(*waits)
        return result


class Gather:
    def __init__(self, part, axis):
        self.axis, self.bit = axis, lax.axis_size(axis) // 2
        self.send(part)

    def send(self, part):
        self.sent = part
        self.got = swapped(part, self.axis, self.bit)

    def advance(self, *waits):
        got = after(self.got, *waits)
        if self.bit == 1:
            return self.sent, got
        self.bit //= 2
        self.send(jnp.concatenate([self.sent, got], axis=1))
        return None

    def finish(self, *waits):
        result = None
        while result is None:
            result = self.advance(*waits)
        return result


def after(value, *others):
    return lax.optimization_barrier((value,) + others)[0] if others else value


class GatherWeights:
    def __init__(self, rows):
        devices = lax.axis_size("fsdp")
        self.rows = rows
        self.side = lax.axis_index("seq") % 2
        half = rows.shape[0] // 2
        self.mine = lax.dynamic_slice_in_dim(rows, self.side * half, half, 0)
        self.got = [
            lax.ppermute(self.mine, "fsdp", [(i, (i + away) % devices) for i in range(devices)])
            for away in range(1, devices)
        ]

    def swap(self, *waits):
        self.got = [after(one, *waits) for one in self.got]
        self.other = [swapped(one, "seq", 1) for one in self.got]

    def result(self, *waits):
        devices = lax.axis_size("fsdp")
        place, side = lax.axis_index("fsdp"), self.side
        count, width = self.rows.shape
        half = (count // 2, width)
        sources = [(place - away) % devices for away in range(devices)]
        where = jnp.stack(sources + [side]).astype(jnp.int32)
        pieces = self.got + [after(one, *waits) for one in self.other]

        def body(where_ref, own_ref, *refs):
            out_ref = refs[-1]
            side = where_ref[devices]
            out_ref[where_ref[0]] = own_ref[...]
            for at in range(1, devices):
                out_ref[where_ref[at], side] = refs[at - 1][...]
                out_ref[where_ref[at], 1 - side] = refs[devices + at - 2][...]

        out = pl.pallas_call(
            body,
            grid_spec=pltpu.PrefetchScalarGridSpec(
                num_scalar_prefetch=1,
                grid=(1,),
                in_specs=[pl.BlockSpec((2,) + half, lambda *_: (0, 0, 0))]
                + [pl.BlockSpec(half, at_origin)] * len(pieces),
                out_specs=pl.BlockSpec((devices, 2) + half, lambda *_: (0, 0, 0, 0)),
            ),
            out_shape=jax.ShapeDtypeStruct((devices, 2) + half, self.rows.dtype),
            compiler_params=kernel_params(1),
            cost_estimate=busy(2.0),
            name="place_weights",
        )(where, self.rows.reshape((2,) + half), *pieces)
        return out.reshape(devices * count, width)


class SmallSum:
    def __init__(self, value):
        self.value = value
        self.left = []
        for axis in ("head", "seq", "fsdp"):
            bit = 1
            while bit < lax.axis_size(axis):
                self.left.append((axis, bit))
                bit *= 2
        self.got = None

    def step(self, *waits):
        if self.got is not None:
            self.value = self.value + after(self.got, *waits)
            self.got = None
        if self.left:
            axis, bit = self.left.pop(0)
            self.got = swapped(self.value, axis, bit)
        return self.value

    def finish(self, *waits):
        while self.got is not None:
            self.step(*waits)
        return self.value


class Reduce:
    def __init__(self, grad):
        self.rows = grad.shape[0]
        self.bit = lax.axis_size("seq") // 2
        self.send(grad)

    def send(self, grad):
        half = grad.shape[0] // 2
        mine = (lax.axis_index("seq") // self.bit) % 2
        self.sent = lax.dynamic_slice_in_dim(grad, (1 - mine) * half, half, 0).astype(BF16)
        self.keep = lax.dynamic_slice_in_dim(grad, mine * half, half, 0)
        self.got = swapped(self.sent, "seq", self.bit)

    def spread(self, *waits):
        grad = self.keep.astype(F32) + after(self.got, *waits).astype(F32)
        while self.bit > 1:
            self.bit //= 2
            self.send(grad)
            grad = self.keep.astype(F32) + self.got.astype(F32)
        devices, place = lax.axis_size("fsdp"), lax.axis_index("fsdp")
        count = grad.shape[0] // devices
        self.total = lax.dynamic_slice_in_dim(grad, place * count, count, 0)
        self.gives, self.gots = [], []
        for away in range(1, devices):
            owner = (place + away) % devices
            give = lax.dynamic_slice_in_dim(grad, owner * count, count, 0).astype(BF16)
            route = [(i, (i + away) % devices) for i in range(devices)]
            self.gives.append(give)
            self.gots.append(lax.ppermute(give, "fsdp", route))

    def finish(self, *waits):
        total = self.total
        for got in self.gots:
            total = total + after(got, *waits).astype(F32)
        return total


def state_from_before(final, trans):
    state = None
    for _ in range(lax.axis_size("seq") - 1):
        sent = final
        if state is not None:
            moved = jnp.einsum("mhij,mhjv->mhiv", trans, state.astype(F32), precision=BEST)
            sent = (final.astype(F32) + moved).astype(BF16)
        state = passed_along(sent, "seq", 1)
    return state


def grad_from_after(first, trans):
    grad = None
    for _ in range(lax.axis_size("seq") - 1):
        sent = first
        if grad is not None:
            moved = jnp.einsum("mhji,mhjv->mhiv", trans, grad.astype(F32), precision=BEST)
            sent = (first.astype(F32) + moved).astype(BF16)
        grad = passed_along(sent, "seq", -1)
    return grad


def rms_unit(values):
    return values * lax.rsqrt(jnp.mean(values * values, axis=-1, keepdims=True) + 1e-05)


def rms_back(values, gain, d_out):
    inv = lax.rsqrt(jnp.mean(values * values, axis=-1, keepdims=True) + 1e-05)
    unit = values * inv
    d_unit = d_out * gain
    d_values = inv * (d_unit - unit * jnp.mean(d_unit * unit, axis=-1, keepdims=True))
    return d_values, d_out * unit


def mat(left, right):
    return lax.dot_general(left, right, (((2,), (0,)), ((), ())), preferred_element_type=F32)


def mat_t(left, right):
    return lax.dot_general(left, right, (((2,), (1,)), ((), ())), preferred_element_type=F32)


def grad_of(left, right):
    left = left.reshape(-1, left.shape[2])
    right = right.reshape(-1, right.shape[2])
    part = lax.dot_general(left, right, (((0,), (0,)), ((), ())), preferred_element_type=F32)
    return part.astype(BF16)


def scatter_grad(grad):
    return lax.psum_scatter(grad, SEQ_FSDP, scatter_dimension=0, tiled=True).astype(F32)


def per_device(
    block_input,
    cotangent,
    doc_lengths,
    attn_gain,
    w_query,
    w_key,
    w_value,
    w_gate,
    w_alpha,
    w_beta,
    conv_query,
    conv_key,
    conv_value,
    a_log,
    dt_bias,
    head_gain,
    w_out,
    mlp_gain,
    w_ffgate,
    w_ffup,
    w_down,
):
    head_devices = lax.axis_size("head")
    seq_devices = lax.axis_size("seq")
    owners = seq_devices * lax.axis_size("fsdp")
    seq_place = lax.axis_index("seq")
    head_place = lax.axis_index("head")
    tok_count, model = block_input.shape[2:]
    row_count = tok_count // head_devices
    row_first = head_place * row_count
    heads = w_query.shape[1] // DK
    hidden_width = w_ffgate.shape[1]
    qw, vw = heads * DK, heads * DV
    rates_at = 2 * qw + vw

    x_own = block_input[:, 0]
    halo = passed_along(x_own[:, tok_count - PAD :], "seq", 1)
    w_first = jnp.concatenate([w_query, w_key, w_value, w_alpha, w_beta], axis=1)
    w_first = jnp.pad(w_first, ((0, 0), (0, LANES - 2 * heads)))
    w_second = jnp.concatenate([w_gate, w_out.T], axis=1)
    w_third = jnp.stack([w_ffgate.T, w_ffup.T, w_down])
    x_pad = jnp.concatenate([halo, x_own], axis=1).astype(F32)
    h_one = (rms_unit(x_pad) * attn_gain).astype(BF16)
    cot = to_slots(cotangent[:, 0], "head")
    slots = slot_table("head")
    first = GatherWeights(w_first)
    first.swap()
    second = GatherWeights(after(w_second, *first.got))
    w_first, h_one, cot, w_third = lax.optimization_barrier(
        (first.result(), h_one, cot, w_third)
    )
    w_third = lax.all_gather(after(w_third, *second.got), "fsdp", axis=0)

    conv_q = lax.dynamic_slice_in_dim(conv_query, head_place * qw, qw, 1)
    conv_k = lax.dynamic_slice_in_dim(conv_key, head_place * qw, qw, 1)
    conv_v = lax.dynamic_slice_in_dim(conv_value, head_place * vw, vw, 1)
    filters = (conv_q, conv_k, conv_v)
    rates = jnp.stack(
        [
            lax.dynamic_slice_in_dim(a_log, head_place * heads, heads, 0),
            lax.dynamic_slice_in_dim(dt_bias, head_place * heads, heads, 0),
        ]
    )
    params = jnp.pad(rates, ((0, 6), (0, LANES - heads)))
    gain_rows = jnp.broadcast_to(head_gain[None], (8, DV))
    lengths = doc_lengths[:, 0]
    docs = lengths.shape[1]
    counted = jnp.arange(docs)[None, :] < jnp.arange(docs + 1)[:, None]
    ends = jnp.sum(jnp.where(counted[None], lengths[:, None, :], 0), axis=2)
    ends = (ends - seq_place * tok_count).astype(jnp.int32)

    micros = range(block_input.shape[0])
    count = len(micros)
    outputs, forwards, gate_backs, backs = (Shared(count) for _ in range(4))
    x_parts = [
        lax.dynamic_slice_in_dim(x_own[m : m + 1], row_first, row_count, 1).astype(F32)
        for m in micros
    ]
    pres, found, saves, transes = {}, {}, {}, {}
    states_in, gates, outs, statess = {}, {}, {}, {}
    attn, rows_two, x_ones, sums, back_sums, back_rows = {}, {}, {}, {}, {}, {}
    y_parts, mlp_terms, d_x_ones = {}, {}, {}
    backed, exts, smalls, gain_sums = {}, {}, {}, {}

    def project(m):
        pres[m] = mat(h_one[m : m + 1], w_first)
        return pres[m]

    def local(m, *waits):
        found[m] = run_local(
            ends[m : m + 1], after(pres[m], *waits), filters, params, heads, seq_devices > 2
        )
        saves[m] = tuple(found[m][:7])
        transes[m] = found[m][8] if seq_devices > 2 else None
        states_in[m] = state_from_before(found[m][7], transes[m])
        return found[m][5]

    def project_gate(m):
        gates[m] = mat(h_one[m : m + 1], w_g)
        return gates[m]

    def output(m, *waits):
        outs[m], statess[m], keep, give = run_output(
            outputs,
            m,
            slots,
            after(states_in[m], *waits),
            saves[m],
            gates[m],
            gain_rows,
            w_second,
        )
        attn[m] = Scatter(keep, give, "head")
        return keep

    def to_feed_forward(m, summed):
        x_ones[m] = x_parts[m] + summed
        rows_two[m] = Gather((rms_unit(x_ones[m]) * mlp_gain).astype(BF16), "head")

    def feed_forward(m, halves, *waits):
        low, high = halves
        keep, give = run_feed_forward(forwards, m, (after(low, *waits), high), cot, w_third)
        sums[m] = Scatter(keep, give, "head")
        return keep

    def to_gate_back(m, both):
        y_parts[m] = (x_ones[m] + both[..., :model]).astype(BF16)
        d_norm, terms = rms_back(x_ones[m], mlp_gain, both[..., model:])
        mlp_terms[m] = jnp.sum(terms, axis=(0, 1))
        d_x_ones[m] = cot[m : m + 1, :row_count].astype(F32) + d_norm
        back_rows[m] = Gather(d_x_ones[m].astype(BF16), "head")

    def gate_back(m, halves, *waits):
        low, high = halves
        d_out, added, grad_first, gain_sum = run_gate_back(
            gate_backs,
            m,
            slots,
            (after(low, *waits), high),
            outs[m],
            gates[m],
            gain_rows,
            saves[m],
            w_second,
        )
        gain_sums[m] = gain_sum
        backed[m] = (d_out, added, grad_from_after(grad_first, transes[m]))
        return gain_sum

    def back(m, *waits):
        d_out, added, grad_incoming = backed[m]
        exts[m], smalls[m] = run_back(
            backs,
            m,
            pres[m],
            filters,
            saves[m],
            statess[m],
            added,
            after(grad_incoming, *waits),
            d_out,
        )
        return smalls[m]

    project(0)
    done = local(0)
    project(1)
    second.swap(done)
    done = local(1, done, *second.got)
    w_second = second.result(done)
    w_g = w_second[:, :vw]
    project_gate(0)
    done = output(0, done)
    moved = project(2)
    attn[0].advance(moved)
    done = local(2, done, attn[0].sent)
    project_gate(1)
    to_feed_forward(0, attn[0].finish(done))
    done = output(1, done, rows_two[0].sent)
    moved = project_gate(2)
    attn[1].advance(moved)
    rows_two[0].advance(done)
    done = output(2, done, attn[1].sent, rows_two[0].sent)
    halves = rows_two[0].finish(done)
    to_feed_forward(1, attn[1].finish(halves[1]))
    attn[2].advance(halves[1])
    done = feed_forward(0, halves, attn[2].sent, rows_two[1].sent)
    rows_two[1].advance(done)
    to_feed_forward(2, attn[2].finish(done))
    halves = rows_two[1].finish(sums[0].sent, rows_two[2].sent)
    sums[0].advance(halves[1])
    done = feed_forward(1, halves, done, sums[0].sent)
    rows_two[2].advance(done)
    to_gate_back(0, sums[0].finish(done))
    halves = rows_two[2].finish(sums[1].sent, back_rows[0].sent)
    sums[1].advance(halves[1])
    back_rows[0].advance(halves[1])
    done = feed_forward(2, halves, done, sums[1].sent, back_rows[0].sent)

    h_two, hid, d_ffg, d_ffu = forwards.arrays
    halves = back_rows[0].finish(done)
    to_gate_back(1, sums[1].finish(done))
    sums[2].advance(done)
    done = gate_back(0, halves, back_rows[1].sent, sums[2].sent)
    back_rows[1].advance(done)
    to_gate_back(2, sums[2].finish(done))
    ff_grads = [
        grad_of(after(d_ffg, done, back_rows[1].sent, back_rows[2].sent), h_two),
        grad_of(d_ffu, h_two),
        grad_of(hid, cot),
    ]
    ff_grads = jnp.stack(ff_grads).reshape(3, hidden_width, owners, -1)
    ff_grads = jnp.transpose(ff_grads, (2, 0, 1, 3))
    halves = back_rows[1].finish(ff_grads)
    back_rows[2].advance(ff_grads)
    done = gate_back(1, halves, back_rows[2].sent, backed[0][2])
    ff_shard = scatter_grad(ff_grads)[0]
    done = back(0, done)
    done = gate_back(2, back_rows[2].finish(done), done, backed[1][2])
    d_gates, d_attn_rows = gate_backs.arrays
    side_grads = jnp.concatenate(
        [grad_of(h_one, d_gates), grad_of(d_attn_rows, outputs.arrays[0])], axis=1
    )
    side = Reduce(side_grads)
    done = back(1, done, side.sent, backed[2][2])
    side.spread(done)

    dx_parts, attn_terms, d_h_sums = {}, {}, {}

    def to_input(m, *waits):
        d_ext, d_gate = exts[m], d_gates[m : m + 1]
        rims = after(passed_along(d_ext[:, :PAD], "seq", -1), *waits)
        d_h_one = mat_t(d_ext[:, PAD:], w_first) + mat_t(d_gate[:, PAD:], w_g)
        d_rim = mat_t(rims, w_first)
        d_h_one = d_h_one + jnp.pad(d_rim, ((0, 0), (tok_count - PAD, 0), (0, 0)))
        unit_own = rms_unit(x_own[m : m + 1].astype(F32))
        attn_terms[m] = jnp.sum(d_h_one * unit_own, axis=(0, 1))
        d_h_one = to_slots(d_h_one.astype(BF16), "head")
        half = tok_count // 2
        d_h_sums[m] = Scatter(d_h_one[:, :half], d_h_one[:, half:], "head")

    def to_end(m, summed):
        d_first, _ = rms_back(x_parts[m], attn_gain, summed)
        dx_parts[m] = d_x_ones[m] + d_first

    to_input(0, done)
    done = back(2, done, *side.gives, d_h_sums[0].sent)
    mix_grad = grad_of(h_one, backs.arrays[0])
    mix = [Reduce(mix_grad[:, : 2 * qw]), Reduce(mix_grad[:, 2 * qw :])]
    to_input(2, mix[0].sent, mix[1].sent)
    to_input(1, mix[0].sent, mix[1].sent)

    small = sum(jnp.sum(one, axis=0) for one in smalls.values())
    rate_sums = small[:2, rates_at : rates_at + heads]
    taps = small[:KCONV]
    sizes = (conv_query.shape[1], conv_key.shape[1], conv_value.shape[1])
    widened = [
        lax.dynamic_update_slice_in_dim(
            jnp.zeros((KCONV, size), F32), taps[:, at : at + width], head_place * width, 1
        )
        for size, at, width in zip(sizes, (0, qw, 2 * qw), (qw, qw, vw))
    ]
    widened_rates = lax.dynamic_update_slice_in_dim(
        jnp.zeros((2, a_log.shape[0]), F32), rate_sums, head_place * heads, 1
    )
    gain_sum = sum(jnp.sum(one[:, 0], axis=0) for one in gain_sums.values())
    pieces = [sum(attn_terms.values()), sum(mlp_terms.values()), gain_sum] + widened + [widened_rates]
    packed = jnp.concatenate([piece.reshape(-1) for piece in pieces])
    length = packed.shape[0]
    packed = jnp.pad(packed, (0, -length % 1024)).reshape(-1, LANES)
    small_sum = SmallSum(packed)
    small_sum.step()
    d_h_sums[0].advance(small_sum.value)
    side_shard = side.finish(small_sum.value)
    ff_shard = [ff_shard[0].T, ff_shard[1].T, ff_shard[2]]
    block_output = jnp.concatenate([y_parts[m] for m in micros])
    mix[0].spread(side_shard, block_output, d_h_sums[0].sent)
    d_h_sums[2].advance(*mix[0].gives)
    d_h_sums[1].advance(*mix[0].gives)
    small_sum.step(*mix[0].gives)
    to_end(0, d_h_sums[0].finish(d_h_sums[1].sent))
    mix[1].spread(small_sum.value, *ff_shard, dx_parts[0])
    small_sum.step(*mix[1].gives)
    to_end(2, d_h_sums[2].finish(small_sum.value))
    to_end(1, d_h_sums[1].finish(small_sum.value))
    input_grad = jnp.concatenate([dx_parts[m] for m in micros])
    small_sum.step(input_grad)
    total = mix[0].finish(small_sum.value)
    small_sum.step(total)
    shard_mix = jnp.concatenate([total, mix[1].finish(small_sum.value)], axis=1)
    packed = small_sum.finish().reshape(-1)
    totals, at = [], 0
    for piece in pieces:
        totals.append(packed[at : at + piece.size].reshape(piece.shape))
        at += piece.size
    tot_attn, tot_mlp, tot_head, tot_cq, tot_ck, tot_cv, tot_rates = totals
    return (
        block_output[:, None],
        input_grad[:, None],
        shard_mix[:, :qw],
        shard_mix[:, qw : 2 * qw],
        shard_mix[:, 2 * qw : rates_at],
        side_shard[:, :vw],
        shard_mix[:, rates_at : rates_at + heads],
        shard_mix[:, rates_at + heads : rates_at + 2 * heads],
        side_shard[:, vw:].T,
        ff_shard[0],
        ff_shard[1],
        ff_shard[2],
        tot_attn,
        tot_mlp,
        tot_head,
        tot_cq,
        tot_ck,
        tot_cv,
        tot_rates[0],
        tot_rates[1],
    )


def solution(mesh):
    rows_by_fsdp = P("fsdp", "head")
    cols_by_fsdp = P("head", "fsdp")
    tokens = P(None, "fsdp", "seq", None)
    return jax.shard_map(
        per_device,
        mesh=mesh,
        in_specs=(
            (tokens, tokens, P(None, "fsdp", None), P())
            + (rows_by_fsdp,) * 6
            + (P(),) * 6
            + (cols_by_fsdp, P(), rows_by_fsdp, rows_by_fsdp, cols_by_fsdp)
        ),
        out_specs=(
            (P(None, "fsdp", ("seq", "head"), None),) * 2
            + (P(SEQ_FSDP, "head"),) * 6
            + (P("head", SEQ_FSDP), P(SEQ_FSDP, "head"), P(SEQ_FSDP, "head"))
            + (P("head", SEQ_FSDP),)
            + (P(),) * 8
        ),
        check_vma=False,
    )
```

```python
import math

import jax
import jax.numpy as jnp
from jax import lax
from jax.experimental import pallas as pl
from jax.experimental.pallas import tpu as pltpu
from jax.sharding import PartitionSpec as P

DK = 128
DV = 256
KCONV = 4
CHUNK = 128
PAD = 16
LANES = 128
FAR = -(1 << 20)

F32 = jnp.float32
BF16 = jnp.bfloat16
BEST = lax.Precision.HIGHEST
SEQ_FSDP = ("seq", "fsdp")


def dot(left, right, left_dim=1, right_dim=0):
    return lax.dot_general(
        left, right, (((left_dim,), (right_dim,)), ((), ())), preferred_element_type=F32
    )


def split_two(value):
    high = value.astype(BF16)
    return high, (value - high.astype(F32)).astype(BF16)


def sigmoid(value):
    return 1.0 / (1.0 + jnp.exp(-value))


def rounded(value):
    return value.astype(BF16).astype(F32)


def row_sum(value):
    return jnp.sum(value, axis=1, keepdims=True)


def twice(value):
    return jnp.concatenate([value, value], axis=1)


def taps_of(padded, since_start):
    taps = [padded[PAD:]]
    for shift in range(1, KCONV):
        moved = pltpu.roll(padded, shift, 0)[PAD:]
        taps.append(jnp.where(since_start >= shift, moved, 0.0))
    return taps


def filtered(taps, filters):
    total = taps[0] * filters[KCONV - 1 : KCONV]
    for shift in range(1, KCONV):
        total = total + taps[shift] * filters[KCONV - 1 - shift : KCONV - shift]
    return total


def unfiltered(grads, filters, since_start):
    zero_rows = jnp.zeros((PAD, grads.shape[1]), F32)
    total = jnp.concatenate([zero_rows, grads * filters[KCONV - 1 : KCONV]], axis=0)
    rows = total.shape[0]
    for shift in range(1, KCONV):
        part = jnp.where(since_start >= shift, grads, 0.0)
        part = part * filters[KCONV - 1 - shift : KCONV - shift]
        part = jnp.concatenate([zero_rows, part], axis=0)
        total = total + pltpu.roll(part, rows - shift, 0)
    return total


def row_of(table, row):
    rows = lax.broadcasted_iota(jnp.int32, table.shape, 0)
    return jnp.sum(jnp.where(rows == row, table, 0.0), axis=0, keepdims=True)


def softplus(value):
    return jnp.maximum(value, 0.0) + jnp.log(1.0 + jnp.exp(-jnp.abs(value)))


def three_parts(value):
    high = value.astype(BF16).astype(F32)
    middle = (value - high).astype(BF16).astype(F32)
    return high, middle, value - high - middle


def stack_rows(rows):
    height = -(-len(rows) // 16) * 16
    place = lax.broadcasted_iota(jnp.int32, (height, rows[0].shape[1]), 0)
    out = jnp.zeros((height, rows[0].shape[1]), F32)
    for at, row in enumerate(rows):
        out = jnp.where(place == at, row, out)
    return out.astype(BF16)


def spread(rows):
    parts = [part for row in rows for part in three_parts(row)]
    stacked = stack_rows(parts)
    shape = (stacked.shape[0], LANES * len(rows))
    place = lax.broadcasted_iota(jnp.int32, shape, 0)
    lane = lax.broadcasted_iota(jnp.int32, shape, 1)
    mine = (place >= (lane // LANES) * 3) & (place < (lane // LANES) * 3 + 3)
    wide = dot(stacked, jnp.where(mine, 1.0, 0.0).astype(BF16), 0, 0)
    return [wide[:, at * LANES : (at + 1) * LANES] for at in range(len(rows))]


def squares_iota():
    rows = lax.broadcasted_iota(jnp.int32, (CHUNK, CHUNK), 0)
    cols = lax.broadcasted_iota(jnp.int32, (CHUNK, CHUNK), 1)
    return rows, cols


def token_rows(ends_ref, logits_ref, params_ref, micro, head, heads, first):
    table = logits_ref[PAD + first : PAD + first + CHUNK, :].T[:8]
    params = params_ref[...]
    lanes = lax.broadcasted_iota(jnp.int32, params.shape, 1)
    params = row_sum(jnp.where(lanes == head, params, 0.0))
    scale = jnp.exp(params[0:1])
    argument = row_of(table, head) + params[1:2]
    beta = sigmoid(row_of(table, heads + head))
    log_decay = -scale * softplus(argument)
    slope = -scale * sigmoid(argument)
    rows, cols = squares_iota()
    upto = jnp.where(rows <= cols, 1.0, 0.0).astype(BF16)
    run = jnp.sum(dot(stack_rows(three_parts(log_decay)), upto), axis=0, keepdims=True)
    position = first + lax.broadcasted_iota(jnp.int32, (1, CHUNK), 1)
    start = jnp.full((1, CHUNK), FAR, jnp.int32)
    for at in range(ends_ref.shape[1]):
        edge = ends_ref[micro, at]
        start = jnp.where(position >= edge, edge, start)
    return beta, log_decay, slope, run, start.astype(F32)


def inverse_unit_lower(stricts):
    rows, cols = squares_iota()
    eye = jnp.where(rows == cols, 1.0, 0.0)

    def corner(width):
        inside = (rows // (2 * width)) == (cols // (2 * width))
        return inside & (rows % (2 * width) >= width) & (cols % (2 * width) < width)

    inverses = [eye - jnp.where(corner(1), strict, 0.0) for strict in stricts]
    width = 2
    while width < CHUNK:
        mask = corner(width)
        held = [inverse.astype(BF16) for inverse in inverses]
        edges = [jnp.where(mask, strict, 0.0).astype(BF16) for strict in stricts]
        lefts = [dot(one, edge).astype(BF16) for one, edge in zip(held, edges)]
        steps = [dot(left, one) for left, one in zip(lefts, held)]
        inverses = [inverse - step for inverse, step in zip(inverses, steps)]
        width *= 2
    out = []
    for strict, inverse in zip(stricts, inverses):
        strict_hi, strict_lo = split_two(strict)
        inv_hi, inv_lo = split_two(inverse)
        product = dot(strict_hi, inv_hi) + dot(strict_hi, inv_lo) + dot(strict_lo, inv_hi)
        out.append((inverse, (eye - inverse - product).astype(BF16), inv_hi))
    return [inverse + dot(inv_hi, miss) for inverse, miss, inv_hi in out]


def decay_terms(run_rows, run_cols, start, first):
    rows, cols = squares_iota()
    allowed = (cols <= rows) & ((cols + first).astype(F32) >= start)
    within = jnp.where(allowed, jnp.exp(jnp.minimum(run_rows - run_cols, 0.0)), 0.0)
    strict = jnp.where(cols < rows, within, 0.0)
    reach = jnp.where(start < first, jnp.exp(run_rows), 0.0)
    last = run_rows[CHUNK - 1 :]
    last_start = start[CHUNK - 1 :]
    tail = jnp.where((rows + first).astype(F32) >= last_start, jnp.exp(last - run_rows), 0.0)
    return within, strict, reach, tail, reach[CHUNK - 1 :]


def ages(starts):
    start = jnp.concatenate(starts, axis=0)
    return lax.broadcasted_iota(jnp.int32, start.shape, 0).astype(F32) - start


def normalized(conved):
    gate = sigmoid(conved)
    active = conved * gate
    inv = lax.rsqrt(row_sum(active * active) + 1e-06)
    return active * inv, inv, gate


def local_kernel(heads, with_trans):
    def body(
        ends_ref, q_ref, k_ref, v_ref, logits_ref, fq_ref, fk_ref, fv_ref, params_ref, *outs
    ):
        qe_ref, ol_ref, mt_ref, nn_ref, ti_ref, rl_ref, rr_ref, fin_ref = outs[:8]
        micro, head = pl.program_id(0), pl.program_id(1)
        rows = q_ref.shape[0] - PAD
        chunks = range(rows // CHUNK)
        parts = [slice(c * CHUNK, (c + 1) * CHUNK) for c in chunks]
        found = [
            token_rows(ends_ref, logits_ref, params_ref, micro, head, heads, c * CHUNK)
            for c in chunks
        ]
        for c in chunks:
            for at, row in enumerate(found[c]):
                rr_ref[at : at + 1, parts[c]] = row
        spreads = [spread([run, beta, start]) for beta, _, _, run, start in found]
        since = ages([one[2] for one in spreads])
        since_wide = twice(since)
        decays = [
            decay_terms(spreads[c][0], found[c][3], spreads[c][2], c * CHUNK) for c in chunks
        ]
        k_conv = filtered(taps_of(rounded(k_ref[...]), since), fk_ref[...])
        keys = normalized(k_conv)[0]
        keys_b = keys.astype(BF16)
        betas = [one[1] for one in spreads]
        grams = [dot(keys_b[part], keys_b[part], 1, 1) for part in parts]
        inverses = inverse_unit_lower(
            [b * decay[1] * gram for b, decay, gram in zip(betas, decays, grams)]
        )
        q_conv = filtered(taps_of(rounded(q_ref[...]), since), fq_ref[...])
        v_conv = filtered(taps_of(rounded(v_ref[...]), since_wide), fv_ref[...])
        queries = normalized(q_conv)[0] * (1.0 / math.sqrt(DK))
        queries_b = queries.astype(BF16)
        values = v_conv * sigmoid(v_conv)
        scores = [dot(queries_b[part], keys_b[part], 1, 1) for part in parts]
        solved = []
        for c, part in zip(chunks, parts):
            within, strict, reach, tail, through = decays[c]
            sides = jnp.concatenate(
                [betas[c] * reach * keys[part], twice(betas[c]) * values[part]], axis=1
            )
            inv_b = inverses[c].astype(BF16)
            ti_ref[part, :] = inv_b
            solved.append(dot(inv_b, sides.astype(BF16)).astype(BF16))
        shifts, adds = [], []
        for c, part in zip(chunks, parts):
            within, strict, reach, tail, through = decays[c]
            out_part = dot((within * scores[c]).astype(BF16), solved[c])
            state_part = dot((tail * keys[part]).astype(BF16), solved[c], 0, 0)
            qe_ref[part, :] = (reach * queries[part] - out_part[:, :DK]).astype(BF16)
            ol_ref[part, :] = out_part[:, DK:]
            shifts.append(state_part[:, :DK].astype(BF16))
            adds.append(state_part[:, DK:])
            mt_ref[part, :] = shifts[c]
            nn_ref[part, :] = adds[c]
            rl_ref[c : c + 1, :] = through
        state = adds[0]
        for c in chunks[1:]:
            moved = dot(shifts[c], state.astype(BF16))
            state = twice(decays[c][4]) * state - moved + adds[c]
        fin_ref[...] = state.astype(fin_ref.dtype)
        if with_trans:
            square_rows, square_cols = squares_iota()
            trans = jnp.where(square_rows == square_cols, 1.0, 0.0)
            for c in chunks:
                trans = decays[c][4] * trans - dot(shifts[c], trans.astype(BF16))
            outs[8][...] = trans

    return body


def slot_of(slots_ref, chunk, per_block):
    first = slots_ref[chunk // per_block] * per_block + chunk % per_block
    return pl.ds(pl.multiple_of(first * CHUNK, CHUNK), CHUNK)


def output_kernel(per_block):
    def body(
        slots_ref,
        inc_ref,
        qe_ref,
        ol_ref,
        mt_ref,
        nn_ref,
        rl_ref,
        gate_ref,
        gain_ref,
        wo_ref,
        og_ref,
        o_ref,
        st_ref,
        keep_ref,
        give_ref,
        sum_scr,
    ):
        rows = qe_ref.shape[0]
        head = pl.program_id(0)
        state = inc_ref[...].astype(F32)
        gain = gain_ref[0:1, :]
        for chunk in range(rows // CHUNK):
            first = chunk * CHUNK
            part = slice(first, first + CHUNK)
            state_b = state.astype(BF16)
            st_ref[part, :] = state_b
            pair = jnp.concatenate([qe_ref[part, :], mt_ref[part, :]], axis=0)
            both = dot(pair, state_b)
            out = both[:CHUNK] + ol_ref[part, :]
            o_ref[part, :] = out
            gate = gate_ref[PAD + first : PAD + first + CHUNK, :].astype(F32)
            norm = lax.rsqrt(jnp.mean(out * out, axis=1, keepdims=True) + 1e-05)
            gated = (out * norm * gain * (gate * sigmoid(gate))).astype(BF16)
            og_ref[slot_of(slots_ref, chunk, per_block), :] = gated
            through = twice(rl_ref[chunk : chunk + 1, :])
            state = through * state - both[CHUNK:] + nn_ref[part, :]
        product = dot(og_ref[...], wo_ref[...], 1, 1)

        @pl.when(head == 0)
        def _():
            sum_scr[...] = product

        @pl.when(head > 0)
        def _():
            sum_scr[...] += product

        @pl.when(head == pl.num_programs(0) - 1)
        def _():
            half = rows // 2
            keep_ref[...] = sum_scr[:half, :].astype(BF16)
            give_ref[...] = sum_scr[half:, :].astype(BF16)

    return body


def gate_back_kernel(per_block):
    def body(
        slots_ref,
        low_ref,
        high_ref,
        o_ref,
        gate_ref,
        gain_ref,
        qe_ref,
        mt_ref,
        rl_ref,
        wo_ref,
        do_ref,
        hg_ref,
        dgate_ref,
        dattn_ref,
        gf_ref,
        gg_ref,
        dog_scr,
    ):
        rows = qe_ref.shape[0]
        gain = gain_ref[0:1, :]
        grad_gain = jnp.zeros((1, DV), F32)
        dgate_ref[:PAD, :] = jnp.zeros((PAD, DV), BF16)
        half = rows // 2
        dog_scr[:half, :] = dot(low_ref[...], wo_ref[...])
        dog_scr[half:, :] = dot(high_ref[...], wo_ref[...])
        state = None
        for chunk in reversed(range(rows // CHUNK)):
            first = chunk * CHUNK
            part = slice(first, first + CHUNK)
            out = o_ref[part, :]
            gate = gate_ref[PAD + first : PAD + first + CHUNK, :].astype(F32)
            dog = dog_scr[slot_of(slots_ref, chunk, per_block), :]
            norm = lax.rsqrt(jnp.mean(out * out, axis=1, keepdims=True) + 1e-05)
            unit = out * norm
            sig = sigmoid(gate)
            swish = gate * sig
            grad_gain = grad_gain + jnp.sum(dog * unit * swish, axis=0, keepdims=True)
            d_gate = dog * unit * gain * (sig * (1.0 + gate * (1.0 - sig)))
            dgate_ref[PAD + first : PAD + first + CHUNK, :] = d_gate.astype(BF16)
            d_unit = dog * gain * swish
            d_out = norm * (d_unit - unit * jnp.mean(d_unit * unit, axis=1, keepdims=True))
            d_out_b = d_out.astype(BF16)
            do_ref[part, :] = d_out_b
            added = dot(qe_ref[part, :], d_out_b, 0, 0)
            hg_ref[part, :] = added
            if state is None:
                state = added
            else:
                moved = dot(mt_ref[part, :], state.astype(BF16), 0, 0)
                state = twice(rl_ref[chunk : chunk + 1, :]) * state - moved + added
        gf_ref[...] = state.astype(gf_ref.dtype)
        first_head = pl.program_id(0) == 0

        @pl.when(first_head)
        def _():
            dattn_ref[:half, :] = low_ref[...]
            dattn_ref[half:, :] = high_ref[...]
            gg_ref[...] = jnp.broadcast_to(grad_gain, gg_ref.shape)

        @pl.when(jnp.logical_not(first_head))
        def _():
            gg_ref[...] += jnp.broadcast_to(grad_gain, gg_ref.shape)

    return body


def feed_forward_kernel(
    low_ref,
    high_ref,
    cot_ref,
    w_ref,
    keep_ref,
    give_ref,
    out_keep_ref,
    out_give_ref,
    h_ref,
    hid_ref,
    dg_ref,
    du_ref,
):
    shards, shard = w_ref.shape[0], w_ref.shape[3]
    half = low_ref.shape[0]
    h_ref[:half, :] = low_ref[...]
    h_ref[half:, :] = high_ref[...]

    def spans(at):
        return slice(at * shard, (at + 1) * shard)

    def entering(ref, which):
        total = None
        for at in range(shards):
            part = dot(ref[:, spans(at)], w_ref[at, which], 1, 1)
            total = part if total is None else total + part
        return total

    gate = entering(h_ref, 0)
    sig = sigmoid(gate)
    swish = gate * sig
    up = entering(h_ref, 1)
    hidden = (swish * up).astype(BF16)
    hid_ref[...] = hidden
    d_hidden = entering(cot_ref, 2)
    d_gate = (d_hidden * up * sig * (1.0 + gate * (1.0 - sig))).astype(BF16)
    d_up = (d_hidden * swish).astype(BF16)
    dg_ref[...] = d_gate
    du_ref[...] = d_up
    for at in range(shards):
        out = dot(hidden, w_ref[at, 2]).astype(BF16)
        d_h = (dot(d_gate, w_ref[at, 0]) + dot(d_up, w_ref[at, 1])).astype(BF16)
        out_keep_ref[:, spans(at)] = out[:half]
        out_give_ref[:, spans(at)] = out[half:]
        keep_ref[:, spans(at)] = d_h[:half]
        give_ref[:, spans(at)] = d_h[half:]


def back_kernel(heads):
    def body(
        q_ref,
        k_ref,
        v_ref,
        rr_ref,
        fq_ref,
        fk_ref,
        fv_ref,
        ti_ref,
        st_ref,
        mt_ref,
        rl_ref,
        hg_ref,
        gin_ref,
        do_ref,
        dext_ref,
        own_ref,
        small_ref,
        dq_scr,
        dk_scr,
        dv_scr,
    ):
        head = pl.program_id(0)
        rows = q_ref.shape[0] - PAD
        logits_at = dext_ref.shape[1] - LANES
        chunks = range(rows // CHUNK)
        parts = [slice(c * CHUNK, (c + 1) * CHUNK) for c in chunks]

        @pl.when(head == 0)
        def _():
            dext_ref[...] = jnp.zeros(dext_ref.shape, BF16)
            small_ref[...] = jnp.zeros(small_ref.shape, F32)

        grads = [None for _ in chunks]
        grad_state = gin_ref[...].astype(F32)
        for c in reversed(chunks):
            grads[c] = grad_state.astype(BF16)
            if c:
                moved = dot(mt_ref[parts[c], :], grads[c], 0, 0)
                through = twice(rl_ref[c : c + 1, :])
                grad_state = through * grad_state - moved + hg_ref[parts[c], :]
        found = [[rr_ref[at : at + 1, part] for at in range(5)] for part in parts]
        spreads = [
            spread([run, beta, start, log_decay, slope])
            for beta, log_decay, slope, run, start in found
        ]
        since = ages([one[2] for one in spreads])
        since_wide = twice(since)
        decays = [
            decay_terms(spreads[c][0], found[c][3], spreads[c][2], c * CHUNK) for c in chunks
        ]
        fq, fk, fv = fq_ref[...], fk_ref[...], fv_ref[...]
        q_taps = taps_of(rounded(q_ref[...]), since)
        k_taps = taps_of(rounded(k_ref[...]), since)
        v_taps = taps_of(rounded(v_ref[...]), since_wide)
        q_conv, k_conv, v_conv = filtered(q_taps, fq), filtered(k_taps, fk), filtered(v_taps, fv)
        q_unit, q_inv, q_gate = normalized(q_conv)
        keys, k_inv, k_gate = normalized(k_conv)
        q_scale = 1.0 / math.sqrt(DK)
        queries = q_unit * q_scale
        v_gate = sigmoid(v_conv)
        values = v_conv * v_gate
        keys_b, queries_b = keys.astype(BF16), queries.astype(BF16)
        square_rows, square_cols = squares_iota()
        later = jnp.where(square_cols >= square_rows, 1.0, 0.0).astype(BF16)
        lanes = lax.broadcasted_iota(jnp.int32, (CHUNK, LANES), 1)
        sums = [jnp.zeros((1, 1), F32), jnp.zeros((1, 1), F32)]
        for c in reversed(chunks):
            part = parts[c]
            within, strict, reach, tail, through = decays[c]
            run, b, start, log_decay, slope = spreads[c]
            k, q, v = keys[part], queries[part], values[part]
            k_b, q_b = keys_b[part], queries_b[part]
            inv_b = ti_ref[part, :]
            state_b = st_ref[part, :]
            grad_b = grads[c]
            d_out = do_ref[part, :]
            gram = dot(k_b, k_b, 1, 1)
            raw = dot(q_b, k_b, 1, 1)
            scores_b = (within * raw).astype(BF16)
            from_both = dot(k_b, jnp.concatenate([state_b, grad_b], axis=1))
            side = twice(b) * (v - twice(reach) * from_both[:, :DV])
            pseudo_b = dot(inv_b, side.astype(BF16)).astype(BF16)
            d_pseudo = dot(scores_b, d_out, 0, 0) + twice(tail) * from_both[:, DV:]
            d_side = dot(inv_b, d_pseudo.astype(BF16), 0, 0)
            d_side_b = d_side.astype(BF16)
            out_and_side = jnp.concatenate([d_out, d_side_b], axis=0)
            squares = dot(out_and_side, pseudo_b, 1, 1)
            by_state = dot(out_and_side, state_b, 1, 1)
            by_grad = dot(pseudo_b, grad_b, 1, 1)
            out_state, side_state = by_state[:CHUNK], by_state[CHUNK:]
            d_raw = within * squares[:CHUNK]
            solve_grad = squares[CHUNK:] * strict
            d_gram = -(b * solve_grad)
            d_raw_b, d_gram_b = d_raw.astype(BF16), d_gram.astype(BF16)
            d_q = reach * out_state + dot(d_raw_b, k_b)
            d_k = tail * by_grad - b * reach * side_state
            d_k = d_k + dot(d_raw_b, q_b, 0, 0) + dot(d_gram_b, k_b) + dot(d_gram_b, k_b, 0, 0)
            dv_scr[part, :] = twice(b) * d_side
            dq_scr[part, :] = d_q
            dk_scr[part, :] = d_k
            side_key = row_sum(k * side_state)
            d_beta = row_sum(d_side * v) - row_sum(solve_grad * gram) - reach * side_key
            weight = d_raw * raw + d_gram * gram
            reach_part = reach * (row_sum(q * out_state) - b * side_key)
            tail_part = tail * row_sum(k * by_grad)
            d_run = row_sum(weight - weight.T) + reach_part - tail_part
            kept = jnp.sum(grad_b.astype(F32) * state_b.astype(F32), axis=0, keepdims=True)
            kept = through * row_sum(kept)
            end_grad = jnp.sum(tail_part, axis=0, keepdims=True) + kept
            run_hi, run_lo = split_two(d_run)
            d_decay = dot(later, run_hi) + dot(later, run_lo) + end_grad
            d_alpha = d_decay * slope
            d_beta_logit = d_beta * b * (1.0 - b)
            sums[0] = sums[0] + jnp.sum((d_decay * log_decay)[:, :1], axis=0, keepdims=True)
            sums[1] = sums[1] + jnp.sum(d_alpha[:, :1], axis=0, keepdims=True)
            place = slice(PAD + c * CHUNK, PAD + (c + 1) * CHUNK)
            held = dext_ref[place, logits_at:].astype(F32)
            held = jnp.where(lanes == head, d_alpha, held)
            held = jnp.where(lanes == heads + head, d_beta_logit, held)
            dext_ref[place, logits_at:] = held.astype(BF16)

        def channel_back(d_conv, taps, filters, since_here, at, width):
            place = pl.ds(pl.multiple_of(at, LANES), width)
            dext_ref[:, place] = unfiltered(d_conv, filters, since_here).astype(BF16)
            for shift in range(KCONV):
                grad = jnp.sum(d_conv * taps[shift], axis=0, keepdims=True)
                small_ref[KCONV - 1 - shift : KCONV - shift, place] = grad

        def unit_back(d_unit, unit, inv, conv, gate):
            d_active = inv * (d_unit - unit * row_sum(d_unit * unit))
            return d_active * gate * (1.0 + conv * (1.0 - gate))

        d_q_conv = unit_back(dq_scr[...] * q_scale, q_unit, q_inv, q_conv, q_gate)
        d_k_conv = unit_back(dk_scr[...], keys, k_inv, k_conv, k_gate)
        d_v_conv = dv_scr[...] * v_gate * (1.0 + v_conv * (1.0 - v_gate))
        channel_back(d_q_conv, q_taps, fq, since, head * DK, DK)
        channel_back(d_k_conv, k_taps, fk, since, (heads + head) * DK, DK)
        channel_back(d_v_conv, v_taps, fv, since_wide, 2 * heads * DK + head * DV, DV)
        rate_rows = lax.broadcasted_iota(jnp.int32, (8, LANES), 0)
        rate_lanes = lax.broadcasted_iota(jnp.int32, (8, LANES), 1)
        rates = jnp.where(rate_rows == 0, sums[0], jnp.where(rate_rows == 1, sums[1], 0.0))
        small_ref[:, logits_at:] += jnp.where(rate_lanes == head, rates, 0.0)

        @pl.when(head == pl.num_programs(0) - 1)
        def _():
            own_ref[...] = dext_ref[...]

    return body


def whole(shape):
    return pl.BlockSpec((None,) + shape, lambda m, h, *_: (m, 0, 0))


def per_head(shape):
    return pl.BlockSpec((None, None) + shape, lambda m, h, *_: (m, h, 0, 0))


def columns(rows, width, skip=0):
    return pl.BlockSpec((None, rows, width), lambda m, h, *_: (m, 0, skip + h))


def filter_cols(width):
    return pl.BlockSpec((KCONV, width), lambda m, h, *_: (0, h))


def fixed(shape):
    return pl.BlockSpec(shape, lambda m, h, *_: (0, 0))


def kernel_params(axes, mebibytes):
    return pltpu.CompilerParams(
        dimension_semantics=("arbitrary",) * axes, vmem_limit_bytes=mebibytes * 1024 * 1024
    )


def busy(microseconds):
    return pl.CostEstimate(
        flops=0, transcendentals=0, bytes_accessed=int(microseconds * 3.3e5)
    )


class Shared:
    def __init__(self, micros):
        self.micros = micros
        self.arrays = None

    def call(
        self, body, micro, grid, prefetch, operands, in_specs, out, scratch, name, cost, mebibytes
    ):
        shared = [at for at, one in enumerate(out) if one[4]]
        held = [] if self.arrays is None else self.arrays
        skip = len(prefetch) + len(operands)

        def wrapped(*refs):
            body(*refs[:skip], *refs[skip + len(held) :])

        out_shape, out_specs = [], []
        for shape, dtype, block, index, is_shared in out:
            leading = (self.micros,) if is_shared else (1,)
            first = micro if is_shared else 0
            place = pltpu.HBM if is_shared else jax.ShapeDtypeStruct
            out_shape.append(place(leading + shape, dtype))
            out_specs.append(
                pl.BlockSpec((None,) + block, lambda *g, i=index, f=first: (f,) + i(*g))
            )
        results = pl.pallas_call(
            wrapped,
            grid_spec=pltpu.PrefetchScalarGridSpec(
                num_scalar_prefetch=len(prefetch),
                grid=grid,
                in_specs=in_specs + [pl.BlockSpec(memory_space=pl.ANY)] * len(held),
                out_specs=out_specs,
                scratch_shapes=scratch,
            ),
            out_shape=out_shape,
            input_output_aliases={skip + at: shared[at] for at in range(len(held))},
            compiler_params=kernel_params(len(grid), mebibytes),
            cost_estimate=busy(cost),
            name=name,
        )(*prefetch, *operands, *held)
        self.arrays = [results[at] for at in shared]
        return [one for at, one in enumerate(results) if at not in shared]


def by_head(h, *_):
    return (h, 0, 0)


def by_column(h, *_):
    return (0, h)


def at_origin(*_):
    return (0, 0)


def mixer_specs(heads, padded):
    return [
        columns(padded, DK),
        columns(padded, DK, heads),
        columns(padded, DV, heads * DK * 2 // DV),
    ]


def filter_specs():
    return [filter_cols(DK), filter_cols(DK), filter_cols(DV)]


def run_local(ends, pre, filters, params, heads, with_trans):
    micros, padded = pre.shape[0], pre.shape[1]
    rows = padded - PAD
    logits_at = pre.shape[2] // LANES - 1
    shapes = [
        ((rows, DK), BF16),
        ((rows, heads * DV), F32),
        ((rows, DK), BF16),
        ((rows, DV), F32),
        ((rows, CHUNK), BF16),
        ((8, LANES), F32),
        ((8, rows), F32),
        ((DK, DV), BF16),
    ]
    if with_trans:
        shapes.append(((DK, DK), F32))
    out_shape, out_specs = [], []
    for at, (shape, dtype) in enumerate(shapes):
        if at == 1:
            out_shape.append(jax.ShapeDtypeStruct((micros,) + shape, dtype))
            out_specs.append(columns(rows, DV))
        else:
            out_shape.append(jax.ShapeDtypeStruct((micros, heads) + shape, dtype))
            out_specs.append(per_head(shape))
    logits_spec = pl.BlockSpec((None, padded, LANES), lambda m, h, *_: (m, 0, logits_at))
    return pl.pallas_call(
        local_kernel(heads, with_trans),
        grid_spec=pltpu.PrefetchScalarGridSpec(
            num_scalar_prefetch=1,
            grid=(micros, heads),
            in_specs=mixer_specs(heads, padded)
            + [logits_spec]
            + filter_specs()
            + [fixed((8, LANES))],
            out_specs=out_specs,
        ),
        out_shape=out_shape,
        compiler_params=kernel_params(2, 12),
        cost_estimate=busy(10.0 * micros),
        name="mixer_local",
    )(ends, pre, pre, pre, pre, *filters, params)


def one_head(shape):
    return pl.BlockSpec((None, None) + shape, lambda h, *_: (0, h, 0, 0))


def one_column(rows, width, skip=0):
    return pl.BlockSpec((None, rows, width), lambda h, *_: (0, 0, skip + h))


def one_whole(shape, micro=0):
    return pl.BlockSpec((None,) + shape, lambda *_: (micro,) + (0,) * len(shape))


def gain_spec():
    return pl.BlockSpec((8, DV), at_origin)


def run_output(shared, micro, slots, incoming, saved, gate, gain, w_out):
    qe, ol, mt, nn, ti, rl, rr = saved
    heads, rows = qe.shape[1:3]
    width = w_out.shape[0]
    half = (rows // 2, width)
    return shared.call(
        output_kernel(rows // slots.shape[0] // CHUNK),
        micro,
        (heads,),
        [slots],
        [incoming, qe, ol, mt, nn, rl, gate, gain, w_out],
        [
            one_head((DK, DV)),
            one_head((rows, DK)),
            one_column(rows, DV),
            one_head((rows, DK)),
            one_head((rows, DV)),
            one_head((8, LANES)),
            one_column(rows + PAD, DV),
            gain_spec(),
            pl.BlockSpec((width, DV), lambda h, *_: (0, heads + h)),
        ],
        [
            ((rows, heads * DV), BF16, (rows, DV), by_column, True),
            ((rows, heads * DV), F32, (rows, DV), by_column, False),
            ((heads, rows, DV), BF16, (None, rows, DV), by_head, False),
            (half, BF16, half, at_origin, False),
            (half, BF16, half, at_origin, False),
        ],
        [pltpu.VMEM((rows, width), F32)],
        "mixer_output",
        6.0,
        14,
    )


def run_gate_back(shared, micro, slots, d_attn, out, gate, gain, saved, w_out):
    qe, ol, mt, nn, ti, rl, rr = saved
    heads, rows = qe.shape[1:3]
    width = w_out.shape[0]
    return shared.call(
        gate_back_kernel(rows // slots.shape[0] // CHUNK),
        micro,
        (heads,),
        [slots],
        [*d_attn, out, gate, gain, qe, mt, rl, w_out],
        [one_whole((rows // 2, width))] * 2
        + [
            one_column(rows, DV),
            one_column(rows + PAD, DV),
            gain_spec(),
            one_head((rows, DK)),
            one_head((rows, DK)),
            one_head((8, LANES)),
            pl.BlockSpec((width, DV), lambda h, *_: (0, heads + h)),
        ],
        [
            ((rows, heads * DV), BF16, (rows, DV), by_column, False),
            ((heads, rows, DV), F32, (None, rows, DV), by_head, False),
            ((rows + PAD, heads * DV), BF16, (rows + PAD, DV), by_column, True),
            ((rows, width), BF16, (rows, width), at_origin, True),
            ((heads, DK, DV), BF16, (None, DK, DV), by_head, False),
            ((8, DV), F32, (8, DV), at_origin, False),
        ],
        [pltpu.VMEM((rows, DV), F32)],
        "mixer_gate_back",
        6.0,
        14,
    )


def run_feed_forward(shared, micro, h_two, cot, weights):
    rows, width = cot.shape[1:]
    hidden = weights.shape[2]
    sums = (rows // 2, width)
    kept = (rows, hidden)
    return shared.call(
        feed_forward_kernel,
        micro,
        (1,),
        [],
        [*h_two, cot, weights],
        [one_whole((rows // 2, width))] * 2
        + [
            one_whole((rows, width), micro),
            pl.BlockSpec(weights.shape, lambda *_: (0, 0, 0, 0)),
        ],
        [
            (sums, BF16, sums, at_origin, False),
            (sums, BF16, sums, at_origin, False),
            (sums, BF16, sums, at_origin, True),
            (sums, BF16, sums, at_origin, True),
            ((rows, width), BF16, (rows, width), at_origin, True),
            (kept, BF16, kept, at_origin, True),
            (kept, BF16, kept, at_origin, True),
            (kept, BF16, kept, at_origin, True),
        ],
        [],
        "feed_forward",
        9.0,
        20,
    )


def run_back(shared, micro, pre, filters, saved, states, added, incoming, d_out):
    qe, ol, mt, nn, ti, rl, rr = saved
    heads, rows = qe.shape[1:3]
    padded = rows + PAD
    width = pre.shape[2]
    return shared.call(
        back_kernel(heads),
        micro,
        (heads,),
        [],
        [pre, pre, pre, rr, *filters, ti, states, mt, rl, added, incoming, d_out],
        [
            one_column(padded, DK),
            one_column(padded, DK, heads),
            one_column(padded, DV, heads * DK * 2 // DV),
            one_head((8, rows)),
            pl.BlockSpec((KCONV, DK), by_column),
            pl.BlockSpec((KCONV, DK), by_column),
            pl.BlockSpec((KCONV, DV), by_column),
            one_head((rows, CHUNK)),
            one_head((rows, DV)),
            one_head((rows, DK)),
            one_head((8, LANES)),
            one_head((rows, DV)),
            one_head((DK, DV)),
            one_column(rows, DV),
        ],
        [
            ((padded, width), BF16, (padded, width), at_origin, True),
            ((padded, width), BF16, (padded, width), at_origin, False),
            ((8, width), F32, (8, width), at_origin, False),
        ],
        [
            pltpu.VMEM((rows, DK), F32),
            pltpu.VMEM((rows, DK), F32),
            pltpu.VMEM((rows, DV), F32),
        ],
        "mixer_back",
        14.0,
        16,
    )


def passed_along(block, axis, distance):
    devices = range(lax.axis_size(axis))
    route = [(i - distance, i) for i in devices if i - distance in devices]
    return lax.ppermute(block, axis, route)


def swapped(block, axis, bit):
    return lax.ppermute(block, axis, [(i, i ^ bit) for i in range(lax.axis_size(axis))])


def reversed_bits(value, size):
    out, bit = 0, 1
    while bit < size:
        out = out * 2 + (value // bit) % 2
        bit *= 2
    return out


def to_slots(rows, axis):
    place = lax.axis_index(axis)
    size = lax.axis_size(axis)
    count = rows.shape[1] // size
    owners = [place ^ reversed_bits(slot, size) for slot in range(size)]
    return jnp.concatenate(
        [lax.dynamic_slice_in_dim(rows, owner * count, count, 1) for owner in owners], axis=1
    )


def slot_table(axis):
    size = lax.axis_size(axis)
    away = jnp.arange(size, dtype=jnp.int32) ^ lax.axis_index(axis)
    return reversed_bits(away, size).astype(jnp.int32)


class Scatter:
    def __init__(self, keep, give, axis):
        self.axis, self.bit, self.keep = axis, 1, keep.astype(F32)
        self.send(give)

    def send(self, give):
        self.sent = give.astype(BF16)
        self.got = swapped(self.sent, self.axis, self.bit)

    def advance(self, *waits):
        parts = self.keep + after(self.got, *waits).astype(F32)
        self.bit *= 2
        if self.bit >= lax.axis_size(self.axis):
            return parts
        half = parts.shape[1] // 2
        self.keep = parts[:, :half]
        self.send(parts[:, half:])
        return None

    def finish(self, *waits):
        result = None
        while result is None:
            result = self.advance(*waits)
        return result


class Gather:
    def __init__(self, part, axis):
        self.axis, self.bit = axis, lax.axis_size(axis) // 2
        self.send(part)

    def send(self, part):
        self.sent = part
        self.got = swapped(part, self.axis, self.bit)

    def advance(self, *waits):
        got = after(self.got, *waits)
        if self.bit == 1:
            return self.sent, got
        self.bit //= 2
        self.send(jnp.concatenate([self.sent, got], axis=1))
        return None

    def finish(self, *waits):
        result = None
        while result is None:
            result = self.advance(*waits)
        return result


def after(value, *others):
    return lax.optimization_barrier((value,) + others)[0] if others else value


class GatherWeights:
    def __init__(self, rows):
        devices = lax.axis_size("fsdp")
        self.rows = rows
        self.side = lax.axis_index("seq") % 2
        half = rows.shape[0] // 2
        self.mine = lax.dynamic_slice_in_dim(rows, self.side * half, half, 0)
        self.got = [
            lax.ppermute(self.mine, "fsdp", [(i, (i + away) % devices) for i in range(devices)])
            for away in range(1, devices)
        ]

    def swap(self, *waits):
        self.got = [after(one, *waits) for one in self.got]
        self.other = [swapped(one, "seq", 1) for one in self.got]

    def result(self, *waits):
        devices = lax.axis_size("fsdp")
        place, side = lax.axis_index("fsdp"), self.side
        count, width = self.rows.shape
        half = (count // 2, width)
        sources = [(place - away) % devices for away in range(devices)]
        where = jnp.stack(sources + [side]).astype(jnp.int32)
        pieces = self.got + [after(one, *waits) for one in self.other]

        def body(where_ref, own_ref, *refs):
            out_ref = refs[-1]
            side = where_ref[devices]
            out_ref[where_ref[0]] = own_ref[...]
            for at in range(1, devices):
                out_ref[where_ref[at], side] = refs[at - 1][...]
                out_ref[where_ref[at], 1 - side] = refs[devices + at - 2][...]

        out = pl.pallas_call(
            body,
            grid_spec=pltpu.PrefetchScalarGridSpec(
                num_scalar_prefetch=1,
                grid=(1,),
                in_specs=[pl.BlockSpec((2,) + half, lambda *_: (0, 0, 0))]
                + [pl.BlockSpec(half, at_origin)] * len(pieces),
                out_specs=pl.BlockSpec((devices, 2) + half, lambda *_: (0, 0, 0, 0)),
            ),
            out_shape=jax.ShapeDtypeStruct((devices, 2) + half, self.rows.dtype),
            compiler_params=kernel_params(1, 12),
            cost_estimate=busy(2.0),
            name="place_weights",
        )(where, self.rows.reshape((2,) + half), *pieces)
        return out.reshape(devices * count, width)


class SmallSum:
    def __init__(self, value):
        self.value = value
        self.left = []
        for axis in ("head", "seq", "fsdp"):
            bit = 1
            while bit < lax.axis_size(axis):
                self.left.append((axis, bit))
                bit *= 2
        self.got = None

    def step(self, *waits):
        if self.got is not None:
            self.value = self.value + after(self.got, *waits)
            self.got = None
        if self.left:
            axis, bit = self.left.pop(0)
            self.got = swapped(self.value, axis, bit)
        return self.value

    def finish(self, *waits):
        while self.got is not None:
            self.step(*waits)
        return self.value


class Reduce:
    def __init__(self, grad):
        self.rows = grad.shape[0]
        self.bit = lax.axis_size("seq") // 2
        self.send(grad)

    def send(self, grad):
        half = grad.shape[0] // 2
        mine = (lax.axis_index("seq") // self.bit) % 2
        self.sent = lax.dynamic_slice_in_dim(grad, (1 - mine) * half, half, 0).astype(BF16)
        self.keep = lax.dynamic_slice_in_dim(grad, mine * half, half, 0)
        self.got = swapped(self.sent, "seq", self.bit)

    def spread(self, *waits):
        grad = self.keep.astype(F32) + after(self.got, *waits).astype(F32)
        while self.bit > 1:
            self.bit //= 2
            self.send(grad)
            grad = self.keep.astype(F32) + self.got.astype(F32)
        devices, place = lax.axis_size("fsdp"), lax.axis_index("fsdp")
        count = grad.shape[0] // devices
        self.total = lax.dynamic_slice_in_dim(grad, place * count, count, 0)
        self.gives, self.gots = [], []
        for away in range(1, devices):
            owner = (place + away) % devices
            give = lax.dynamic_slice_in_dim(grad, owner * count, count, 0).astype(BF16)
            route = [(i, (i + away) % devices) for i in range(devices)]
            self.gives.append(give)
            self.gots.append(lax.ppermute(give, "fsdp", route))

    def finish(self, *waits):
        total = self.total
        for got in self.gots:
            total = total + after(got, *waits).astype(F32)
        return total


def state_from_before(final, trans):
    state = None
    for _ in range(lax.axis_size("seq") - 1):
        sent = final
        if state is not None:
            moved = jnp.einsum("mhij,mhjv->mhiv", trans, state.astype(F32), precision=BEST)
            sent = (final.astype(F32) + moved).astype(BF16)
        state = passed_along(sent, "seq", 1)
    return state


def grad_from_after(first, trans):
    grad = None
    for _ in range(lax.axis_size("seq") - 1):
        sent = first
        if grad is not None:
            moved = jnp.einsum("mhji,mhjv->mhiv", trans, grad.astype(F32), precision=BEST)
            sent = (first.astype(F32) + moved).astype(BF16)
        grad = passed_along(sent, "seq", -1)
    return grad


def rms_unit(values):
    return values * lax.rsqrt(jnp.mean(values * values, axis=-1, keepdims=True) + 1e-05)


def rms_back(values, gain, d_out):
    inv = lax.rsqrt(jnp.mean(values * values, axis=-1, keepdims=True) + 1e-05)
    unit = values * inv
    d_unit = d_out * gain
    d_values = inv * (d_unit - unit * jnp.mean(d_unit * unit, axis=-1, keepdims=True))
    return d_values, d_out * unit


def mat(left, right):
    return lax.dot_general(left, right, (((2,), (0,)), ((), ())), preferred_element_type=F32)


def mat_t(left, right):
    return lax.dot_general(left, right, (((2,), (1,)), ((), ())), preferred_element_type=F32)


def grad_of(left, right):
    left = left.reshape(-1, left.shape[2])
    right = right.reshape(-1, right.shape[2])
    part = lax.dot_general(left, right, (((0,), (0,)), ((), ())), preferred_element_type=F32)
    return part.astype(BF16)


def scatter_grad(grad):
    return lax.psum_scatter(grad, SEQ_FSDP, scatter_dimension=0, tiled=True).astype(F32)


def per_device(
    block_input,
    cotangent,
    doc_lengths,
    attn_gain,
    w_query,
    w_key,
    w_value,
    w_gate,
    w_alpha,
    w_beta,
    conv_query,
    conv_key,
    conv_value,
    a_log,
    dt_bias,
    head_gain,
    w_out,
    mlp_gain,
    w_ffgate,
    w_ffup,
    w_down,
):
    head_devices = lax.axis_size("head")
    seq_devices = lax.axis_size("seq")
    owners = seq_devices * lax.axis_size("fsdp")
    seq_place = lax.axis_index("seq")
    head_place = lax.axis_index("head")
    tok_count, model = block_input.shape[2:]
    row_count = tok_count // head_devices
    row_first = head_place * row_count
    heads = w_query.shape[1] // DK
    hidden_width = w_ffgate.shape[1]
    qw, vw = heads * DK, heads * DV
    rates_at = 2 * qw + vw

    x_own = block_input[:, 0]
    halo = passed_along(x_own[:, tok_count - PAD :], "seq", 1)
    w_first = jnp.concatenate([w_query, w_key, w_value, w_alpha, w_beta], axis=1)
    w_first = jnp.pad(w_first, ((0, 0), (0, LANES - 2 * heads)))
    w_second = jnp.concatenate([w_gate, w_out.T], axis=1)
    w_third = jnp.stack([w_ffgate.T, w_ffup.T, w_down])
    x_pad = jnp.concatenate([halo, x_own], axis=1).astype(F32)
    h_one = (rms_unit(x_pad) * attn_gain).astype(BF16)
    cot = to_slots(cotangent[:, 0], "head")
    slots = slot_table("head")
    first = GatherWeights(w_first)
    first.swap()
    second = GatherWeights(after(w_second, first.other[0]))
    w_first, h_one, cot = lax.optimization_barrier((first.result(), h_one, cot))

    conv_q = lax.dynamic_slice_in_dim(conv_query, head_place * qw, qw, 1)
    conv_k = lax.dynamic_slice_in_dim(conv_key, head_place * qw, qw, 1)
    conv_v = lax.dynamic_slice_in_dim(conv_value, head_place * vw, vw, 1)
    filters = (conv_q, conv_k, conv_v)
    rates = jnp.stack(
        [
            lax.dynamic_slice_in_dim(a_log, head_place * heads, heads, 0),
            lax.dynamic_slice_in_dim(dt_bias, head_place * heads, heads, 0),
        ]
    )
    params = jnp.pad(rates, ((0, 6), (0, LANES - heads)))
    gain_rows = jnp.broadcast_to(head_gain[None], (8, DV))
    lengths = doc_lengths[:, 0]
    docs = lengths.shape[1]
    counted = jnp.arange(docs)[None, :] < jnp.arange(docs + 1)[:, None]
    ends = jnp.sum(jnp.where(counted[None], lengths[:, None, :], 0), axis=2)
    ends = (ends - seq_place * tok_count).astype(jnp.int32)

    micros = range(block_input.shape[0])
    count = len(micros)
    outputs, forwards, gate_backs, backs = (Shared(count) for _ in range(4))
    x_parts = [
        lax.dynamic_slice_in_dim(x_own[m : m + 1], row_first, row_count, 1).astype(F32)
        for m in micros
    ]
    pres, found, saves, transes = {}, {}, {}, {}
    states_in, gates, outs, statess = {}, {}, {}, {}
    attn, rows_two, x_ones, sums, back_sums, back_rows = {}, {}, {}, {}, {}, {}
    mlp_terms, d_x_ones = {}, {}
    backed, exts, smalls, gain_sums = {}, {}, {}, {}

    def project(m):
        pres[m] = mat(h_one[m : m + 1], w_first)
        return pres[m]

    def local(m, *waits):
        found[m] = run_local(
            ends[m : m + 1], after(pres[m], *waits), filters, params, heads, seq_devices > 2
        )
        saves[m] = tuple(found[m][:7])
        transes[m] = found[m][8] if seq_devices > 2 else None
        states_in[m] = state_from_before(found[m][7], transes[m])
        return found[m][5]

    def project_gate(m):
        gates[m] = mat(h_one[m : m + 1], w_g)
        return gates[m]

    def output(m, *waits):
        outs[m], statess[m], keep, give = run_output(
            outputs,
            m,
            slots,
            after(states_in[m], *waits),
            saves[m],
            gates[m],
            gain_rows,
            w_second,
        )
        attn[m] = Scatter(keep, give, "head")
        return keep

    def to_feed_forward(m, summed):
        x_ones[m] = x_parts[m] + summed
        rows_two[m] = Gather((rms_unit(x_ones[m]) * mlp_gain).astype(BF16), "head")

    def feed_forward(m, halves, *waits):
        low, high = halves
        keep, give = run_feed_forward(forwards, m, (after(low, *waits), high), cot, w_third)
        sums[m] = Scatter(keep, give, "head")
        return keep

    def to_gate_back(m, summed):
        d_norm, terms = rms_back(x_ones[m], mlp_gain, summed)
        mlp_terms[m] = jnp.sum(terms, axis=(0, 1))
        d_x_ones[m] = cot[m : m + 1, :row_count].astype(F32) + d_norm
        back_rows[m] = Gather(d_x_ones[m].astype(BF16), "head")

    def gate_back(m, halves, *waits):
        low, high = halves
        d_out, added, grad_first, gain_sum = run_gate_back(
            gate_backs,
            m,
            slots,
            (after(low, *waits), high),
            outs[m],
            gates[m],
            gain_rows,
            saves[m],
            w_second,
        )
        gain_sums[m] = gain_sum
        backed[m] = (d_out, added, grad_from_after(grad_first, transes[m]))
        return gain_sum

    def back(m, *waits):
        d_out, added, grad_incoming = backed[m]
        exts[m], smalls[m] = run_back(
            backs,
            m,
            pres[m],
            filters,
            saves[m],
            statess[m],
            added,
            after(grad_incoming, *waits),
            d_out,
        )
        return smalls[m]

    project(0)
    done = local(0)
    second.swap(done)
    w_third = lax.all_gather(after(w_third, *second.got), "fsdp", axis=0)
    project(1)
    done = local(1, done)
    w_second = second.result(done)
    w_g = w_second[:, :vw]
    project_gate(0)
    done = output(0, done)
    project(2)
    done = local(2, done)
    attn[0].advance(done)
    project_gate(1)
    done = output(1, done, attn[0].sent)
    to_feed_forward(0, attn[0].finish(done))
    project_gate(2)
    done = output(2, done, rows_two[0].sent)
    attn[1].advance(done)
    rows_two[0].advance(attn[1].sent)
    attn[2].advance(rows_two[0].sent)
    done = feed_forward(0, rows_two[0].finish(attn[2].sent))
    to_feed_forward(1, attn[1].finish(done))
    to_feed_forward(2, attn[2].finish(rows_two[1].sent))
    sums[0].advance(rows_two[2].sent)
    rows_two[1].advance(sums[0].sent)
    done = feed_forward(1, rows_two[1].finish(rows_two[1].sent))
    rows_two[2].advance(done)
    sums[1].advance(rows_two[2].sent)
    to_gate_back(0, sums[0].finish(sums[1].sent))
    done = feed_forward(2, rows_two[2].finish(back_rows[0].sent))
    out_keep, out_give, h_two, hid, d_ffg, d_ffu = forwards.arrays
    grad_gate = grad_of(after(d_ffg, done), h_two)
    sums[2].advance(grad_gate)
    back_rows[0].advance(sums[2].sent)
    grad_up = grad_of(after(d_ffu, back_rows[0].sent), h_two)
    to_gate_back(1, sums[1].finish(grad_up))
    grad_down = grad_of(after(hid, back_rows[1].sent), cot)
    done = gate_back(0, back_rows[0].finish(grad_down))
    back_rows[1].advance(done)
    to_gate_back(2, sums[2].finish(back_rows[1].sent))
    ff_grads = jnp.stack([after(grad_gate, back_rows[2].sent), grad_up, grad_down])
    ff_grads = ff_grads.reshape(3, hidden_width, owners, -1)
    ff_grads = jnp.transpose(ff_grads, (2, 0, 1, 3))
    ff_shard = scatter_grad(ff_grads)[0]
    done = gate_back(1, back_rows[1].finish(ff_grads))
    back_rows[2].advance(done)
    done = back(0, back_rows[2].sent)
    done = gate_back(2, back_rows[2].finish(done), backed[1][2])
    out_sum = Scatter(after(out_keep, done), out_give, "head")
    d_gates, d_attn_rows = gate_backs.arrays
    side_grads = jnp.concatenate(
        [grad_of(h_one, d_gates), grad_of(d_attn_rows, outputs.arrays[0])], axis=1
    )
    side = Reduce(side_grads)
    dx_parts, attn_terms, d_h_sums = {}, {}, {}

    def to_input(m, *waits):
        d_ext, d_gate = exts[m], d_gates[m : m + 1]
        rims = after(passed_along(d_ext[:, :PAD], "seq", -1), *waits)
        d_h_one = mat_t(d_ext[:, PAD:], w_first) + mat_t(d_gate[:, PAD:], w_g)
        d_rim = mat_t(rims, w_first)
        d_h_one = d_h_one + jnp.pad(d_rim, ((0, 0), (tok_count - PAD, 0), (0, 0)))
        unit_own = rms_unit(x_own[m : m + 1].astype(F32))
        attn_terms[m] = jnp.sum(d_h_one * unit_own, axis=(0, 1))
        d_h_one = to_slots(d_h_one.astype(BF16), "head")
        half = tok_count // 2
        d_h_sums[m] = Scatter(d_h_one[:, :half], d_h_one[:, half:], "head")

    def to_end(m, summed):
        d_first, _ = rms_back(x_parts[m], attn_gain, summed)
        dx_parts[m] = d_x_ones[m] + d_first

    done = back(1, done, side.sent, backed[2][2], out_sum.sent)
    to_input(0, done)
    to_input(1, d_h_sums[0].sent)
    out_sum.advance(d_h_sums[1].sent)
    side.spread(out_sum.sent)
    d_h_sums[0].advance(*side.gives)
    done = back(2, done, *side.gives, d_h_sums[0].sent, ff_shard)
    x_all = jnp.concatenate([x_ones[m] for m in micros])
    block_output = (x_all + out_sum.finish(done)).astype(BF16)
    mix_grad = grad_of(h_one, backs.arrays[0])
    mix = [Reduce(mix_grad[:, : 2 * qw]), Reduce(mix_grad[:, 2 * qw :])]
    to_input(2, mix[0].sent, mix[1].sent)
    d_h_sums[1].advance(d_h_sums[2].sent)

    small = sum(jnp.sum(one, axis=0) for one in smalls.values())
    rate_sums = small[:2, rates_at : rates_at + heads]
    taps = small[:KCONV]
    sizes = (conv_query.shape[1], conv_key.shape[1], conv_value.shape[1])
    widened = [
        lax.dynamic_update_slice_in_dim(
            jnp.zeros((KCONV, size), F32), taps[:, at : at + width], head_place * width, 1
        )
        for size, at, width in zip(sizes, (0, qw, 2 * qw), (qw, qw, vw))
    ]
    widened_rates = lax.dynamic_update_slice_in_dim(
        jnp.zeros((2, a_log.shape[0]), F32), rate_sums, head_place * heads, 1
    )
    gain_sum = sum(jnp.sum(one[:, 0], axis=0) for one in gain_sums.values())
    pieces = [sum(attn_terms.values()), sum(mlp_terms.values()), gain_sum] + widened + [widened_rates]
    packed = jnp.concatenate([piece.reshape(-1) for piece in pieces])
    length = packed.shape[0]
    packed = jnp.pad(packed, (0, -length % 1024)).reshape(-1, LANES)
    small_sum = SmallSum(packed)
    small_sum.step()
    side_shard = side.finish(small_sum.value)
    small_sum.step(side_shard)
    to_end(0, d_h_sums[0].finish(small_sum.value))
    ff_shard = [ff_shard[0].T, ff_shard[1].T, ff_shard[2]]
    mix[0].spread(side_shard, block_output, dx_parts[0])
    d_h_sums[2].advance(*mix[0].gives)
    small_sum.step(*mix[0].gives)
    to_end(1, d_h_sums[1].finish(small_sum.value))
    mix[1].spread(small_sum.value, *ff_shard, dx_parts[1])
    small_sum.step(*mix[1].gives)
    to_end(2, d_h_sums[2].finish(small_sum.value))
    input_grad = jnp.concatenate([dx_parts[m] for m in micros])
    total = mix[0].finish(input_grad)
    shard_mix = jnp.concatenate([total, mix[1].finish(total)], axis=1)
    packed = small_sum.finish().reshape(-1)
    totals, at = [], 0
    for piece in pieces:
        totals.append(packed[at : at + piece.size].reshape(piece.shape))
        at += piece.size
    tot_attn, tot_mlp, tot_head, tot_cq, tot_ck, tot_cv, tot_rates = totals
    return (
        block_output[:, None],
        input_grad[:, None],
        shard_mix[:, :qw],
        shard_mix[:, qw : 2 * qw],
        shard_mix[:, 2 * qw : rates_at],
        side_shard[:, :vw],
        shard_mix[:, rates_at : rates_at + heads],
        shard_mix[:, rates_at + heads : rates_at + 2 * heads],
        side_shard[:, vw:].T,
        ff_shard[0],
        ff_shard[1],
        ff_shard[2],
        tot_attn,
        tot_mlp,
        tot_head,
        tot_cq,
        tot_ck,
        tot_cv,
        tot_rates[0],
        tot_rates[1],
    )


def solution(mesh):
    rows_by_fsdp = P("fsdp", "head")
    cols_by_fsdp = P("head", "fsdp")
    tokens = P(None, "fsdp", "seq", None)
    return jax.shard_map(
        per_device,
        mesh=mesh,
        in_specs=(
            (tokens, tokens, P(None, "fsdp", None), P())
            + (rows_by_fsdp,) * 6
            + (P(),) * 6
            + (cols_by_fsdp, P(), rows_by_fsdp, rows_by_fsdp, cols_by_fsdp)
        ),
        out_specs=(
            (P(None, "fsdp", ("seq", "head"), None),) * 2
            + (P(SEQ_FSDP, "head"),) * 6
            + (P("head", SEQ_FSDP), P(SEQ_FSDP, "head"), P(SEQ_FSDP, "head"))
            + (P("head", SEQ_FSDP),)
            + (P(),) * 8
        ),
        check_vma=False,
    )
```

```python
import math

import jax
import jax.numpy as jnp
from jax import lax
from jax.experimental import pallas as pl
from jax.experimental.pallas import tpu as pltpu
from jax.sharding import PartitionSpec as P

DK = 128
DV = 256
KCONV = 4
CHUNK = 128
PAD = 16
LANES = 128
FAR = -(1 << 20)

F32 = jnp.float32
BF16 = jnp.bfloat16
BEST = lax.Precision.HIGHEST
SEQ_FSDP = ("seq", "fsdp")


def dot(left, right, left_dim=1, right_dim=0):
    return lax.dot_general(
        left, right, (((left_dim,), (right_dim,)), ((), ())), preferred_element_type=F32
    )


def split_two(value):
    high = value.astype(BF16)
    return high, (value - high.astype(F32)).astype(BF16)


def sigmoid(value):
    return 1.0 / (1.0 + jnp.exp(-value))


def rounded(value):
    return value.astype(BF16).astype(F32)


def row_sum(value):
    return jnp.sum(value, axis=1, keepdims=True)


def twice(value):
    return jnp.concatenate([value, value], axis=1)


def taps_of(padded, since_start):
    taps = [padded[PAD:]]
    for shift in range(1, KCONV):
        moved = pltpu.roll(padded, shift, 0)[PAD:]
        taps.append(jnp.where(since_start >= shift, moved, 0.0))
    return taps


def filtered(taps, filters):
    total = taps[0] * filters[KCONV - 1 : KCONV]
    for shift in range(1, KCONV):
        total = total + taps[shift] * filters[KCONV - 1 - shift : KCONV - shift]
    return total


def unfiltered(grads, filters, since_start):
    zero_rows = jnp.zeros((PAD, grads.shape[1]), F32)
    total = jnp.concatenate([zero_rows, grads * filters[KCONV - 1 : KCONV]], axis=0)
    rows = total.shape[0]
    for shift in range(1, KCONV):
        part = jnp.where(since_start >= shift, grads, 0.0)
        part = part * filters[KCONV - 1 - shift : KCONV - shift]
        part = jnp.concatenate([zero_rows, part], axis=0)
        total = total + pltpu.roll(part, rows - shift, 0)
    return total


def row_of(table, row):
    rows = lax.broadcasted_iota(jnp.int32, table.shape, 0)
    return jnp.sum(jnp.where(rows == row, table, 0.0), axis=0, keepdims=True)


def softplus(value):
    return jnp.maximum(value, 0.0) + jnp.log(1.0 + jnp.exp(-jnp.abs(value)))


def three_parts(value):
    high = value.astype(BF16).astype(F32)
    middle = (value - high).astype(BF16).astype(F32)
    return high, middle, value - high - middle


def stack_rows(rows):
    height = -(-len(rows) // 16) * 16
    place = lax.broadcasted_iota(jnp.int32, (height, rows[0].shape[1]), 0)
    out = jnp.zeros((height, rows[0].shape[1]), F32)
    for at, row in enumerate(rows):
        out = jnp.where(place == at, row, out)
    return out.astype(BF16)


def spread(rows):
    parts = [part for row in rows for part in three_parts(row)]
    stacked = stack_rows(parts)
    shape = (stacked.shape[0], LANES * len(rows))
    place = lax.broadcasted_iota(jnp.int32, shape, 0)
    lane = lax.broadcasted_iota(jnp.int32, shape, 1)
    mine = (place >= (lane // LANES) * 3) & (place < (lane // LANES) * 3 + 3)
    wide = dot(stacked, jnp.where(mine, 1.0, 0.0).astype(BF16), 0, 0)
    return [wide[:, at * LANES : (at + 1) * LANES] for at in range(len(rows))]


def squares_iota():
    rows = lax.broadcasted_iota(jnp.int32, (CHUNK, CHUNK), 0)
    cols = lax.broadcasted_iota(jnp.int32, (CHUNK, CHUNK), 1)
    return rows, cols


def token_rows(ends_ref, logits_ref, params_ref, micro, head, heads, first):
    table = logits_ref[PAD + first : PAD + first + CHUNK, :].T[:8]
    params = params_ref[...]
    lanes = lax.broadcasted_iota(jnp.int32, params.shape, 1)
    params = row_sum(jnp.where(lanes == head, params, 0.0))
    scale = jnp.exp(params[0:1])
    argument = row_of(table, head) + params[1:2]
    beta = sigmoid(row_of(table, heads + head))
    log_decay = -scale * softplus(argument)
    slope = -scale * sigmoid(argument)
    rows, cols = squares_iota()
    upto = jnp.where(rows <= cols, 1.0, 0.0).astype(BF16)
    run = jnp.sum(dot(stack_rows(three_parts(log_decay)), upto), axis=0, keepdims=True)
    position = first + lax.broadcasted_iota(jnp.int32, (1, CHUNK), 1)
    start = jnp.full((1, CHUNK), FAR, jnp.int32)
    for at in range(ends_ref.shape[1]):
        edge = ends_ref[micro, at]
        start = jnp.where(position >= edge, edge, start)
    return beta, log_decay, slope, run, start.astype(F32)


def inverse_unit_lower(stricts):
    rows, cols = squares_iota()
    eye = jnp.where(rows == cols, 1.0, 0.0)

    def corner(width):
        inside = (rows // (2 * width)) == (cols // (2 * width))
        return inside & (rows % (2 * width) >= width) & (cols % (2 * width) < width)

    inverses = [eye - jnp.where(corner(1), strict, 0.0) for strict in stricts]
    width = 2
    while width < CHUNK:
        mask = corner(width)
        held = [inverse.astype(BF16) for inverse in inverses]
        edges = [jnp.where(mask, strict, 0.0).astype(BF16) for strict in stricts]
        lefts = [dot(one, edge).astype(BF16) for one, edge in zip(held, edges)]
        steps = [dot(left, one) for left, one in zip(lefts, held)]
        inverses = [inverse - step for inverse, step in zip(inverses, steps)]
        width *= 2
    out = []
    for strict, inverse in zip(stricts, inverses):
        strict_hi, strict_lo = split_two(strict)
        inv_hi, inv_lo = split_two(inverse)
        product = dot(strict_hi, inv_hi) + dot(strict_hi, inv_lo) + dot(strict_lo, inv_hi)
        out.append((inverse, (eye - inverse - product).astype(BF16), inv_hi))
    return [inverse + dot(inv_hi, miss) for inverse, miss, inv_hi in out]


def decay_terms(run_rows, run_cols, start, first):
    rows, cols = squares_iota()
    allowed = (cols <= rows) & ((cols + first).astype(F32) >= start)
    within = jnp.where(allowed, jnp.exp(jnp.minimum(run_rows - run_cols, 0.0)), 0.0)
    strict = jnp.where(cols < rows, within, 0.0)
    reach = jnp.where(start < first, jnp.exp(run_rows), 0.0)
    last = run_rows[CHUNK - 1 :]
    last_start = start[CHUNK - 1 :]
    tail = jnp.where((rows + first).astype(F32) >= last_start, jnp.exp(last - run_rows), 0.0)
    return within, strict, reach, tail, reach[CHUNK - 1 :]


def ages(starts):
    start = jnp.concatenate(starts, axis=0)
    return lax.broadcasted_iota(jnp.int32, start.shape, 0).astype(F32) - start


def normalized(conved):
    gate = sigmoid(conved)
    active = conved * gate
    inv = lax.rsqrt(row_sum(active * active) + 1e-06)
    return active * inv, inv, gate


def local_kernel(heads, with_trans):
    def body(
        ends_ref, q_ref, k_ref, v_ref, logits_ref, fq_ref, fk_ref, fv_ref, params_ref, *outs
    ):
        qe_ref, ol_ref, mt_ref, nn_ref, ti_ref, rl_ref, rr_ref, fin_ref = outs[:8]
        micro, head = pl.program_id(0), pl.program_id(1)
        rows = q_ref.shape[0] - PAD
        chunks = range(rows // CHUNK)
        parts = [slice(c * CHUNK, (c + 1) * CHUNK) for c in chunks]
        found = [
            token_rows(ends_ref, logits_ref, params_ref, micro, head, heads, c * CHUNK)
            for c in chunks
        ]
        for c in chunks:
            for at, row in enumerate(found[c]):
                rr_ref[at : at + 1, parts[c]] = row
        spreads = [spread([run, beta, start]) for beta, _, _, run, start in found]
        since = ages([one[2] for one in spreads])
        since_wide = twice(since)
        decays = [
            decay_terms(spreads[c][0], found[c][3], spreads[c][2], c * CHUNK) for c in chunks
        ]
        k_conv = filtered(taps_of(rounded(k_ref[...]), since), fk_ref[...])
        keys = normalized(k_conv)[0]
        keys_b = keys.astype(BF16)
        betas = [one[1] for one in spreads]
        grams = [dot(keys_b[part], keys_b[part], 1, 1) for part in parts]
        inverses = inverse_unit_lower(
            [b * decay[1] * gram for b, decay, gram in zip(betas, decays, grams)]
        )
        q_conv = filtered(taps_of(rounded(q_ref[...]), since), fq_ref[...])
        v_conv = filtered(taps_of(rounded(v_ref[...]), since_wide), fv_ref[...])
        queries = normalized(q_conv)[0] * (1.0 / math.sqrt(DK))
        queries_b = queries.astype(BF16)
        values = v_conv * sigmoid(v_conv)
        scores = [dot(queries_b[part], keys_b[part], 1, 1) for part in parts]
        solved = []
        for c, part in zip(chunks, parts):
            within, strict, reach, tail, through = decays[c]
            sides = jnp.concatenate(
                [betas[c] * reach * keys[part], twice(betas[c]) * values[part]], axis=1
            )
            inv_b = inverses[c].astype(BF16)
            ti_ref[part, :] = inv_b
            solved.append(dot(inv_b, sides.astype(BF16)).astype(BF16))
        shifts, adds = [], []
        for c, part in zip(chunks, parts):
            within, strict, reach, tail, through = decays[c]
            out_part = dot((within * scores[c]).astype(BF16), solved[c])
            state_part = dot((tail * keys[part]).astype(BF16), solved[c], 0, 0)
            qe_ref[part, :] = (reach * queries[part] - out_part[:, :DK]).astype(BF16)
            ol_ref[part, :] = out_part[:, DK:]
            shifts.append(state_part[:, :DK].astype(BF16))
            adds.append(state_part[:, DK:])
            mt_ref[part, :] = shifts[c]
            nn_ref[part, :] = adds[c]
            rl_ref[c : c + 1, :] = through
        state = adds[0]
        for c in chunks[1:]:
            moved = dot(shifts[c], state.astype(BF16))
            state = twice(decays[c][4]) * state - moved + adds[c]
        fin_ref[...] = state.astype(fin_ref.dtype)
        if with_trans:
            square_rows, square_cols = squares_iota()
            trans = jnp.where(square_rows == square_cols, 1.0, 0.0)
            for c in chunks:
                trans = decays[c][4] * trans - dot(shifts[c], trans.astype(BF16))
            outs[8][...] = trans

    return body


def slot_of(slots_ref, chunk, per_block):
    first = slots_ref[chunk // per_block] * per_block + chunk % per_block
    return pl.ds(pl.multiple_of(first * CHUNK, CHUNK), CHUNK)


def output_kernel(per_block):
    def body(
        slots_ref,
        inc_ref,
        qe_ref,
        ol_ref,
        mt_ref,
        nn_ref,
        rl_ref,
        gate_ref,
        gain_ref,
        wo_ref,
        og_ref,
        o_ref,
        st_ref,
        keep_ref,
        give_ref,
        sum_scr,
    ):
        rows = qe_ref.shape[0]
        head = pl.program_id(0)
        state = inc_ref[...].astype(F32)
        gain = gain_ref[0:1, :]
        for chunk in range(rows // CHUNK):
            first = chunk * CHUNK
            part = slice(first, first + CHUNK)
            state_b = state.astype(BF16)
            st_ref[part, :] = state_b
            pair = jnp.concatenate([qe_ref[part, :], mt_ref[part, :]], axis=0)
            both = dot(pair, state_b)
            out = both[:CHUNK] + ol_ref[part, :]
            o_ref[part, :] = out
            gate = gate_ref[PAD + first : PAD + first + CHUNK, :].astype(F32)
            norm = lax.rsqrt(jnp.mean(out * out, axis=1, keepdims=True) + 1e-05)
            gated = (out * norm * gain * (gate * sigmoid(gate))).astype(BF16)
            og_ref[slot_of(slots_ref, chunk, per_block), :] = gated
            through = twice(rl_ref[chunk : chunk + 1, :])
            state = through * state - both[CHUNK:] + nn_ref[part, :]
        product = dot(og_ref[...], wo_ref[...], 1, 1)

        @pl.when(head == 0)
        def _():
            sum_scr[...] = product

        @pl.when(head > 0)
        def _():
            sum_scr[...] += product

        @pl.when(head == pl.num_programs(0) - 1)
        def _():
            half = rows // 2
            keep_ref[...] = sum_scr[:half, :].astype(BF16)
            give_ref[...] = sum_scr[half:, :].astype(BF16)

    return body


def gate_back_kernel(per_block):
    def body(
        slots_ref,
        low_ref,
        high_ref,
        o_ref,
        gate_ref,
        gain_ref,
        qe_ref,
        mt_ref,
        rl_ref,
        wo_ref,
        do_ref,
        hg_ref,
        dgate_ref,
        dattn_ref,
        gf_ref,
        gg_ref,
        dog_scr,
    ):
        rows = qe_ref.shape[0]
        gain = gain_ref[0:1, :]
        grad_gain = jnp.zeros((1, DV), F32)
        dgate_ref[:PAD, :] = jnp.zeros((PAD, DV), BF16)
        half = rows // 2
        dog_scr[:half, :] = dot(low_ref[...], wo_ref[...])
        dog_scr[half:, :] = dot(high_ref[...], wo_ref[...])
        state = None
        for chunk in reversed(range(rows // CHUNK)):
            first = chunk * CHUNK
            part = slice(first, first + CHUNK)
            out = o_ref[part, :]
            gate = gate_ref[PAD + first : PAD + first + CHUNK, :].astype(F32)
            dog = dog_scr[slot_of(slots_ref, chunk, per_block), :]
            norm = lax.rsqrt(jnp.mean(out * out, axis=1, keepdims=True) + 1e-05)
            unit = out * norm
            sig = sigmoid(gate)
            swish = gate * sig
            grad_gain = grad_gain + jnp.sum(dog * unit * swish, axis=0, keepdims=True)
            d_gate = dog * unit * gain * (sig * (1.0 + gate * (1.0 - sig)))
            dgate_ref[PAD + first : PAD + first + CHUNK, :] = d_gate.astype(BF16)
            d_unit = dog * gain * swish
            d_out = norm * (d_unit - unit * jnp.mean(d_unit * unit, axis=1, keepdims=True))
            d_out_b = d_out.astype(BF16)
            do_ref[part, :] = d_out_b
            added = dot(qe_ref[part, :], d_out_b, 0, 0)
            hg_ref[part, :] = added
            if state is None:
                state = added
            else:
                moved = dot(mt_ref[part, :], state.astype(BF16), 0, 0)
                state = twice(rl_ref[chunk : chunk + 1, :]) * state - moved + added
        gf_ref[...] = state.astype(gf_ref.dtype)
        first_head = pl.program_id(0) == 0

        @pl.when(first_head)
        def _():
            dattn_ref[:half, :] = low_ref[...]
            dattn_ref[half:, :] = high_ref[...]
            gg_ref[...] = jnp.broadcast_to(grad_gain, gg_ref.shape)

        @pl.when(jnp.logical_not(first_head))
        def _():
            gg_ref[...] += jnp.broadcast_to(grad_gain, gg_ref.shape)

    return body


def feed_forward_kernel(
    low_ref,
    high_ref,
    cot_ref,
    w_ref,
    keep_ref,
    give_ref,
    out_keep_ref,
    out_give_ref,
    h_ref,
    hid_ref,
    dg_ref,
    du_ref,
):
    shards, shard = w_ref.shape[0], w_ref.shape[3]
    half = low_ref.shape[0]
    h_ref[:half, :] = low_ref[...]
    h_ref[half:, :] = high_ref[...]

    def spans(at):
        return slice(at * shard, (at + 1) * shard)

    def entering(ref, which):
        total = None
        for at in range(shards):
            part = dot(ref[:, spans(at)], w_ref[at, which], 1, 1)
            total = part if total is None else total + part
        return total

    gate = entering(h_ref, 0)
    sig = sigmoid(gate)
    swish = gate * sig
    up = entering(h_ref, 1)
    hidden = (swish * up).astype(BF16)
    hid_ref[...] = hidden
    d_hidden = entering(cot_ref, 2)
    d_gate = (d_hidden * up * sig * (1.0 + gate * (1.0 - sig))).astype(BF16)
    d_up = (d_hidden * swish).astype(BF16)
    dg_ref[...] = d_gate
    du_ref[...] = d_up
    for at in range(shards):
        out = dot(hidden, w_ref[at, 2]).astype(BF16)
        d_h = (dot(d_gate, w_ref[at, 0]) + dot(d_up, w_ref[at, 1])).astype(BF16)
        out_keep_ref[:, spans(at)] = out[:half]
        out_give_ref[:, spans(at)] = out[half:]
        keep_ref[:, spans(at)] = d_h[:half]
        give_ref[:, spans(at)] = d_h[half:]


def back_kernel(heads):
    def body(
        q_ref,
        k_ref,
        v_ref,
        rr_ref,
        fq_ref,
        fk_ref,
        fv_ref,
        ti_ref,
        st_ref,
        mt_ref,
        rl_ref,
        hg_ref,
        gin_ref,
        do_ref,
        dext_ref,
        own_ref,
        small_ref,
        dq_scr,
        dk_scr,
        dv_scr,
    ):
        head = pl.program_id(0)
        rows = q_ref.shape[0] - PAD
        logits_at = dext_ref.shape[1] - LANES
        chunks = range(rows // CHUNK)
        parts = [slice(c * CHUNK, (c + 1) * CHUNK) for c in chunks]

        @pl.when(head == 0)
        def _():
            dext_ref[...] = jnp.zeros(dext_ref.shape, BF16)
            small_ref[...] = jnp.zeros(small_ref.shape, F32)

        grads = [None for _ in chunks]
        grad_state = gin_ref[...].astype(F32)
        for c in reversed(chunks):
            grads[c] = grad_state.astype(BF16)
            if c:
                moved = dot(mt_ref[parts[c], :], grads[c], 0, 0)
                through = twice(rl_ref[c : c + 1, :])
                grad_state = through * grad_state - moved + hg_ref[parts[c], :]
        found = [[rr_ref[at : at + 1, part] for at in range(5)] for part in parts]
        spreads = [
            spread([run, beta, start, log_decay, slope])
            for beta, log_decay, slope, run, start in found
        ]
        since = ages([one[2] for one in spreads])
        since_wide = twice(since)
        decays = [
            decay_terms(spreads[c][0], found[c][3], spreads[c][2], c * CHUNK) for c in chunks
        ]
        fq, fk, fv = fq_ref[...], fk_ref[...], fv_ref[...]
        q_taps = taps_of(rounded(q_ref[...]), since)
        k_taps = taps_of(rounded(k_ref[...]), since)
        v_taps = taps_of(rounded(v_ref[...]), since_wide)
        q_conv, k_conv, v_conv = filtered(q_taps, fq), filtered(k_taps, fk), filtered(v_taps, fv)
        q_unit, q_inv, q_gate = normalized(q_conv)
        keys, k_inv, k_gate = normalized(k_conv)
        q_scale = 1.0 / math.sqrt(DK)
        queries = q_unit * q_scale
        v_gate = sigmoid(v_conv)
        values = v_conv * v_gate
        keys_b, queries_b = keys.astype(BF16), queries.astype(BF16)
        square_rows, square_cols = squares_iota()
        later = jnp.where(square_cols >= square_rows, 1.0, 0.0).astype(BF16)
        lanes = lax.broadcasted_iota(jnp.int32, (CHUNK, LANES), 1)
        sums = [jnp.zeros((1, 1), F32), jnp.zeros((1, 1), F32)]
        for c in reversed(chunks):
            part = parts[c]
            within, strict, reach, tail, through = decays[c]
            run, b, start, log_decay, slope = spreads[c]
            k, q, v = keys[part], queries[part], values[part]
            k_b, q_b = keys_b[part], queries_b[part]
            inv_b = ti_ref[part, :]
            state_b = st_ref[part, :]
            grad_b = grads[c]
            d_out = do_ref[part, :]
            gram = dot(k_b, k_b, 1, 1)
            raw = dot(q_b, k_b, 1, 1)
            scores_b = (within * raw).astype(BF16)
            from_both = dot(k_b, jnp.concatenate([state_b, grad_b], axis=1))
            side = twice(b) * (v - twice(reach) * from_both[:, :DV])
            pseudo_b = dot(inv_b, side.astype(BF16)).astype(BF16)
            d_pseudo = dot(scores_b, d_out, 0, 0) + twice(tail) * from_both[:, DV:]
            d_side = dot(inv_b, d_pseudo.astype(BF16), 0, 0)
            d_side_b = d_side.astype(BF16)
            out_and_side = jnp.concatenate([d_out, d_side_b], axis=0)
            squares = dot(out_and_side, pseudo_b, 1, 1)
            by_state = dot(out_and_side, state_b, 1, 1)
            by_grad = dot(pseudo_b, grad_b, 1, 1)
            out_state, side_state = by_state[:CHUNK], by_state[CHUNK:]
            d_raw = within * squares[:CHUNK]
            solve_grad = squares[CHUNK:] * strict
            d_gram = -(b * solve_grad)
            d_raw_b, d_gram_b = d_raw.astype(BF16), d_gram.astype(BF16)
            d_q = reach * out_state + dot(d_raw_b, k_b)
            d_k = tail * by_grad - b * reach * side_state
            d_k = d_k + dot(d_raw_b, q_b, 0, 0) + dot(d_gram_b, k_b) + dot(d_gram_b, k_b, 0, 0)
            dv_scr[part, :] = twice(b) * d_side
            dq_scr[part, :] = d_q
            dk_scr[part, :] = d_k
            side_key = row_sum(k * side_state)
            d_beta = row_sum(d_side * v) - row_sum(solve_grad * gram) - reach * side_key
            weight = d_raw * raw + d_gram * gram
            reach_part = reach * (row_sum(q * out_state) - b * side_key)
            tail_part = tail * row_sum(k * by_grad)
            d_run = row_sum(weight - weight.T) + reach_part - tail_part
            kept = jnp.sum(grad_b.astype(F32) * state_b.astype(F32), axis=0, keepdims=True)
            kept = through * row_sum(kept)
            end_grad = jnp.sum(tail_part, axis=0, keepdims=True) + kept
            run_hi, run_lo = split_two(d_run)
            d_decay = dot(later, run_hi) + dot(later, run_lo) + end_grad
            d_alpha = d_decay * slope
            d_beta_logit = d_beta * b * (1.0 - b)
            sums[0] = sums[0] + jnp.sum((d_decay * log_decay)[:, :1], axis=0, keepdims=True)
            sums[1] = sums[1] + jnp.sum(d_alpha[:, :1], axis=0, keepdims=True)
            place = slice(PAD + c * CHUNK, PAD + (c + 1) * CHUNK)
            held = dext_ref[place, logits_at:].astype(F32)
            held = jnp.where(lanes == head, d_alpha, held)
            held = jnp.where(lanes == heads + head, d_beta_logit, held)
            dext_ref[place, logits_at:] = held.astype(BF16)

        def channel_back(d_conv, taps, filters, since_here, at, width):
            place = pl.ds(pl.multiple_of(at, LANES), width)
            dext_ref[:, place] = unfiltered(d_conv, filters, since_here).astype(BF16)
            for shift in range(KCONV):
                grad = jnp.sum(d_conv * taps[shift], axis=0, keepdims=True)
                small_ref[KCONV - 1 - shift : KCONV - shift, place] = grad

        def unit_back(d_unit, unit, inv, conv, gate):
            d_active = inv * (d_unit - unit * row_sum(d_unit * unit))
            return d_active * gate * (1.0 + conv * (1.0 - gate))

        d_q_conv = unit_back(dq_scr[...] * q_scale, q_unit, q_inv, q_conv, q_gate)
        d_k_conv = unit_back(dk_scr[...], keys, k_inv, k_conv, k_gate)
        d_v_conv = dv_scr[...] * v_gate * (1.0 + v_conv * (1.0 - v_gate))
        channel_back(d_q_conv, q_taps, fq, since, head * DK, DK)
        channel_back(d_k_conv, k_taps, fk, since, (heads + head) * DK, DK)
        channel_back(d_v_conv, v_taps, fv, since_wide, 2 * heads * DK + head * DV, DV)
        rate_rows = lax.broadcasted_iota(jnp.int32, (8, LANES), 0)
        rate_lanes = lax.broadcasted_iota(jnp.int32, (8, LANES), 1)
        rates = jnp.where(rate_rows == 0, sums[0], jnp.where(rate_rows == 1, sums[1], 0.0))
        small_ref[:, logits_at:] += jnp.where(rate_lanes == head, rates, 0.0)

        @pl.when(head == pl.num_programs(0) - 1)
        def _():
            own_ref[...] = dext_ref[...]

    return body


def whole(shape):
    return pl.BlockSpec((None,) + shape, lambda m, h, *_: (m, 0, 0))


def per_head(shape):
    return pl.BlockSpec((None, None) + shape, lambda m, h, *_: (m, h, 0, 0))


def columns(rows, width, skip=0):
    return pl.BlockSpec((None, rows, width), lambda m, h, *_: (m, 0, skip + h))


def filter_cols(width):
    return pl.BlockSpec((KCONV, width), lambda m, h, *_: (0, h))


def fixed(shape):
    return pl.BlockSpec(shape, lambda m, h, *_: (0, 0))


def kernel_params(axes, mebibytes):
    return pltpu.CompilerParams(
        dimension_semantics=("arbitrary",) * axes, vmem_limit_bytes=mebibytes * 1024 * 1024
    )


def busy(microseconds):
    return pl.CostEstimate(
        flops=0, transcendentals=0, bytes_accessed=int(microseconds * 3.3e5)
    )


class Shared:
    def __init__(self, micros):
        self.micros = micros
        self.arrays = None

    def call(
        self, body, micro, grid, prefetch, operands, in_specs, out, scratch, name, cost, mebibytes
    ):
        shared = [at for at, one in enumerate(out) if one[4]]
        held = [] if self.arrays is None else self.arrays
        skip = len(prefetch) + len(operands)

        def wrapped(*refs):
            body(*refs[:skip], *refs[skip + len(held) :])

        out_shape, out_specs = [], []
        for shape, dtype, block, index, is_shared in out:
            leading = (self.micros,) if is_shared else (1,)
            first = micro if is_shared else 0
            place = pltpu.HBM if is_shared else jax.ShapeDtypeStruct
            out_shape.append(place(leading + shape, dtype))
            out_specs.append(
                pl.BlockSpec((None,) + block, lambda *g, i=index, f=first: (f,) + i(*g))
            )
        results = pl.pallas_call(
            wrapped,
            grid_spec=pltpu.PrefetchScalarGridSpec(
                num_scalar_prefetch=len(prefetch),
                grid=grid,
                in_specs=in_specs + [pl.BlockSpec(memory_space=pl.ANY)] * len(held),
                out_specs=out_specs,
                scratch_shapes=scratch,
            ),
            out_shape=out_shape,
            input_output_aliases={skip + at: shared[at] for at in range(len(held))},
            compiler_params=kernel_params(len(grid), mebibytes),
            cost_estimate=busy(cost),
            name=name,
        )(*prefetch, *operands, *held)
        self.arrays = [results[at] for at in shared]
        return [one for at, one in enumerate(results) if at not in shared]


def by_head(h, *_):
    return (h, 0, 0)


def by_column(h, *_):
    return (0, h)


def at_origin(*_):
    return (0, 0)


def mixer_specs(heads, padded):
    return [
        columns(padded, DK),
        columns(padded, DK, heads),
        columns(padded, DV, heads * DK * 2 // DV),
    ]


def filter_specs():
    return [filter_cols(DK), filter_cols(DK), filter_cols(DV)]


def run_local(ends, pre, filters, params, heads, with_trans):
    micros, padded = pre.shape[0], pre.shape[1]
    rows = padded - PAD
    logits_at = pre.shape[2] // LANES - 1
    shapes = [
        ((rows, DK), BF16),
        ((rows, heads * DV), F32),
        ((rows, DK), BF16),
        ((rows, DV), F32),
        ((rows, CHUNK), BF16),
        ((8, LANES), F32),
        ((8, rows), F32),
        ((DK, DV), BF16),
    ]
    if with_trans:
        shapes.append(((DK, DK), F32))
    out_shape, out_specs = [], []
    for at, (shape, dtype) in enumerate(shapes):
        if at == 1:
            out_shape.append(jax.ShapeDtypeStruct((micros,) + shape, dtype))
            out_specs.append(columns(rows, DV))
        else:
            out_shape.append(jax.ShapeDtypeStruct((micros, heads) + shape, dtype))
            out_specs.append(per_head(shape))
    logits_spec = pl.BlockSpec((None, padded, LANES), lambda m, h, *_: (m, 0, logits_at))
    return pl.pallas_call(
        local_kernel(heads, with_trans),
        grid_spec=pltpu.PrefetchScalarGridSpec(
            num_scalar_prefetch=1,
            grid=(micros, heads),
            in_specs=mixer_specs(heads, padded)
            + [logits_spec]
            + filter_specs()
            + [fixed((8, LANES))],
            out_specs=out_specs,
        ),
        out_shape=out_shape,
        compiler_params=kernel_params(2, 10),
        cost_estimate=busy(10.0 * micros),
        name="mixer_local",
    )(ends, pre, pre, pre, pre, *filters, params)


def one_head(shape):
    return pl.BlockSpec((None, None) + shape, lambda h, *_: (0, h, 0, 0))


def one_column(rows, width, skip=0):
    return pl.BlockSpec((None, rows, width), lambda h, *_: (0, 0, skip + h))


def one_whole(shape, micro=0):
    return pl.BlockSpec((None,) + shape, lambda *_: (micro,) + (0,) * len(shape))


def gain_spec():
    return pl.BlockSpec((8, DV), at_origin)


def run_output(shared, micro, slots, incoming, saved, gate, gain, w_out):
    qe, ol, mt, nn, ti, rl, rr = saved
    heads, rows = qe.shape[1:3]
    width = w_out.shape[0]
    half = (rows // 2, width)
    return shared.call(
        output_kernel(rows // slots.shape[0] // CHUNK),
        micro,
        (heads,),
        [slots],
        [incoming, qe, ol, mt, nn, rl, gate, gain, w_out],
        [
            one_head((DK, DV)),
            one_head((rows, DK)),
            one_column(rows, DV),
            one_head((rows, DK)),
            one_head((rows, DV)),
            one_head((8, LANES)),
            one_column(rows + PAD, DV),
            gain_spec(),
            pl.BlockSpec((width, DV), lambda h, *_: (0, heads + h)),
        ],
        [
            ((rows, heads * DV), BF16, (rows, DV), by_column, True),
            ((rows, heads * DV), F32, (rows, DV), by_column, False),
            ((heads, rows, DV), BF16, (None, rows, DV), by_head, False),
            (half, BF16, half, at_origin, False),
            (half, BF16, half, at_origin, False),
        ],
        [pltpu.VMEM((rows, width), F32)],
        "mixer_output",
        6.0,
        14,
    )


def run_gate_back(shared, micro, slots, d_attn, out, gate, gain, saved, w_out):
    qe, ol, mt, nn, ti, rl, rr = saved
    heads, rows = qe.shape[1:3]
    width = w_out.shape[0]
    return shared.call(
        gate_back_kernel(rows // slots.shape[0] // CHUNK),
        micro,
        (heads,),
        [slots],
        [*d_attn, out, gate, gain, qe, mt, rl, w_out],
        [one_whole((rows // 2, width))] * 2
        + [
            one_column(rows, DV),
            one_column(rows + PAD, DV),
            gain_spec(),
            one_head((rows, DK)),
            one_head((rows, DK)),
            one_head((8, LANES)),
            pl.BlockSpec((width, DV), lambda h, *_: (0, heads + h)),
        ],
        [
            ((rows, heads * DV), BF16, (rows, DV), by_column, False),
            ((heads, rows, DV), F32, (None, rows, DV), by_head, False),
            ((rows + PAD, heads * DV), BF16, (rows + PAD, DV), by_column, True),
            ((rows, width), BF16, (rows, width), at_origin, True),
            ((heads, DK, DV), BF16, (None, DK, DV), by_head, False),
            ((8, DV), F32, (8, DV), at_origin, False),
        ],
        [pltpu.VMEM((rows, DV), F32)],
        "mixer_gate_back",
        6.0,
        14,
    )


def run_feed_forward(shared, micro, h_two, cot, weights):
    rows, width = cot.shape[1:]
    hidden = weights.shape[2]
    sums = (rows // 2, width)
    kept = (rows, hidden)
    return shared.call(
        feed_forward_kernel,
        micro,
        (1,),
        [],
        [*h_two, cot, weights],
        [one_whole((rows // 2, width))] * 2
        + [
            one_whole((rows, width), micro),
            pl.BlockSpec(weights.shape, lambda *_: (0, 0, 0, 0)),
        ],
        [
            (sums, BF16, sums, at_origin, False),
            (sums, BF16, sums, at_origin, False),
            (sums, BF16, sums, at_origin, True),
            (sums, BF16, sums, at_origin, True),
            ((rows, width), BF16, (rows, width), at_origin, True),
            (kept, BF16, kept, at_origin, True),
            (kept, BF16, kept, at_origin, True),
            (kept, BF16, kept, at_origin, True),
        ],
        [],
        "feed_forward",
        9.0,
        17,
    )


def run_back(shared, micro, pre, filters, saved, states, added, incoming, d_out):
    qe, ol, mt, nn, ti, rl, rr = saved
    heads, rows = qe.shape[1:3]
    padded = rows + PAD
    width = pre.shape[2]
    return shared.call(
        back_kernel(heads),
        micro,
        (heads,),
        [],
        [pre, pre, pre, rr, *filters, ti, states, mt, rl, added, incoming, d_out],
        [
            one_column(padded, DK),
            one_column(padded, DK, heads),
            one_column(padded, DV, heads * DK * 2 // DV),
            one_head((8, rows)),
            pl.BlockSpec((KCONV, DK), by_column),
            pl.BlockSpec((KCONV, DK), by_column),
            pl.BlockSpec((KCONV, DV), by_column),
            one_head((rows, CHUNK)),
            one_head((rows, DV)),
            one_head((rows, DK)),
            one_head((8, LANES)),
            one_head((rows, DV)),
            one_head((DK, DV)),
            one_column(rows, DV),
        ],
        [
            ((padded, width), BF16, (padded, width), at_origin, True),
            ((padded, width), BF16, (padded, width), at_origin, False),
            ((8, width), F32, (8, width), at_origin, False),
        ],
        [
            pltpu.VMEM((rows, DK), F32),
            pltpu.VMEM((rows, DK), F32),
            pltpu.VMEM((rows, DV), F32),
        ],
        "mixer_back",
        14.0,
        16,
    )


def passed_along(block, axis, distance):
    devices = range(lax.axis_size(axis))
    route = [(i - distance, i) for i in devices if i - distance in devices]
    return lax.ppermute(block, axis, route)


def swapped(block, axis, bit):
    return lax.ppermute(block, axis, [(i, i ^ bit) for i in range(lax.axis_size(axis))])


def reversed_bits(value, size):
    out, bit = 0, 1
    while bit < size:
        out = out * 2 + (value // bit) % 2
        bit *= 2
    return out


def to_slots(rows, axis):
    place = lax.axis_index(axis)
    size = lax.axis_size(axis)
    count = rows.shape[1] // size
    owners = [place ^ reversed_bits(slot, size) for slot in range(size)]
    return jnp.concatenate(
        [lax.dynamic_slice_in_dim(rows, owner * count, count, 1) for owner in owners], axis=1
    )


def slot_table(axis):
    size = lax.axis_size(axis)
    away = jnp.arange(size, dtype=jnp.int32) ^ lax.axis_index(axis)
    return reversed_bits(away, size).astype(jnp.int32)


class Scatter:
    def __init__(self, keep, give, axis):
        self.axis, self.bit, self.keep = axis, 1, keep.astype(F32)
        self.send(give)

    def send(self, give):
        self.sent = give.astype(BF16)
        self.got = swapped(self.sent, self.axis, self.bit)

    def advance(self, *waits):
        parts = self.keep + after(self.got, *waits).astype(F32)
        self.bit *= 2
        if self.bit >= lax.axis_size(self.axis):
            return parts
        half = parts.shape[1] // 2
        self.keep = parts[:, :half]
        self.send(parts[:, half:])
        return None

    def finish(self, *waits):
        result = None
        while result is None:
            result = self.advance(*waits)
        return result


class Gather:
    def __init__(self, part, axis):
        self.axis, self.bit = axis, lax.axis_size(axis) // 2
        self.send(part)

    def send(self, part):
        self.sent = part
        self.got = swapped(part, self.axis, self.bit)

    def advance(self, *waits):
        got = after(self.got, *waits)
        if self.bit == 1:
            return self.sent, got
        self.bit //= 2
        self.send(jnp.concatenate([self.sent, got], axis=1))
        return None

    def finish(self, *waits):
        result = None
        while result is None:
            result = self.advance(*waits)
        return result


def after(value, *others):
    return lax.optimization_barrier((value,) + others)[0] if others else value


class GatherWeights:
    def __init__(self, rows):
        devices = lax.axis_size("fsdp")
        self.rows = rows
        self.side = lax.axis_index("seq") % 2
        half = rows.shape[0] // 2
        self.mine = lax.dynamic_slice_in_dim(rows, self.side * half, half, 0)
        self.got = [
            lax.ppermute(self.mine, "fsdp", [(i, (i + away) % devices) for i in range(devices)])
            for away in range(1, devices)
        ]

    def swap(self, *waits):
        self.got = [after(one, *waits) for one in self.got]
        self.other = [swapped(one, "seq", 1) for one in self.got]

    def result(self, *waits):
        devices = lax.axis_size("fsdp")
        place, side = lax.axis_index("fsdp"), self.side
        count, width = self.rows.shape
        half = (count // 2, width)
        sources = [(place - away) % devices for away in range(devices)]
        where = jnp.stack(sources + [side]).astype(jnp.int32)
        pieces = self.got + [after(one, *waits) for one in self.other]

        def body(where_ref, own_ref, *refs):
            out_ref = refs[-1]
            side = where_ref[devices]
            out_ref[where_ref[0]] = own_ref[...]
            for at in range(1, devices):
                out_ref[where_ref[at], side] = refs[at - 1][...]
                out_ref[where_ref[at], 1 - side] = refs[devices + at - 2][...]

        out = pl.pallas_call(
            body,
            grid_spec=pltpu.PrefetchScalarGridSpec(
                num_scalar_prefetch=1,
                grid=(1,),
                in_specs=[pl.BlockSpec((2,) + half, lambda *_: (0, 0, 0))]
                + [pl.BlockSpec(half, at_origin)] * len(pieces),
                out_specs=pl.BlockSpec((devices, 2) + half, lambda *_: (0, 0, 0, 0)),
            ),
            out_shape=jax.ShapeDtypeStruct((devices, 2) + half, self.rows.dtype),
            compiler_params=kernel_params(1, 12),
            cost_estimate=busy(2.0),
            name="place_weights",
        )(where, self.rows.reshape((2,) + half), *pieces)
        return out.reshape(devices * count, width)


class SmallSum:
    def __init__(self, value):
        self.value = value
        self.left = ["head", "seq", "fsdp"]
        self.got = []

    def step(self, *waits):
        for got in self.got:
            self.value = self.value + after(got, *waits)
        self.got = []
        if self.left:
            axis = self.left.pop(0)
            devices = lax.axis_size(axis)
            self.got = [
                lax.ppermute(self.value, axis, [(i, (i + away) % devices) for i in range(devices)])
                for away in range(1, devices)
            ]
        return self.value

    def finish(self, *waits):
        while self.got:
            self.step(*waits)
        return self.value


class Reduce:
    def __init__(self, grad):
        self.rows = grad.shape[0]
        self.bit = lax.axis_size("seq") // 2
        self.send(grad)

    def send(self, grad):
        half = grad.shape[0] // 2
        mine = (lax.axis_index("seq") // self.bit) % 2
        self.sent = lax.dynamic_slice_in_dim(grad, (1 - mine) * half, half, 0).astype(BF16)
        self.keep = lax.dynamic_slice_in_dim(grad, mine * half, half, 0)
        self.got = swapped(self.sent, "seq", self.bit)

    def spread(self, *waits):
        grad = self.keep.astype(F32) + after(self.got, *waits).astype(F32)
        while self.bit > 1:
            self.bit //= 2
            self.send(grad)
            grad = self.keep.astype(F32) + self.got.astype(F32)
        devices, place = lax.axis_size("fsdp"), lax.axis_index("fsdp")
        count = grad.shape[0] // devices
        self.total = lax.dynamic_slice_in_dim(grad, place * count, count, 0)
        self.gives, self.gots = [], []
        for away in range(1, devices):
            owner = (place + away) % devices
            give = lax.dynamic_slice_in_dim(grad, owner * count, count, 0).astype(BF16)
            route = [(i, (i + away) % devices) for i in range(devices)]
            self.gives.append(give)
            self.gots.append(lax.ppermute(give, "fsdp", route))

    def finish(self, *waits):
        total = self.total
        for got in self.gots:
            total = total + after(got, *waits).astype(F32)
        return total


def state_from_before(final, trans):
    state = None
    for _ in range(lax.axis_size("seq") - 1):
        sent = final
        if state is not None:
            moved = jnp.einsum("mhij,mhjv->mhiv", trans, state.astype(F32), precision=BEST)
            sent = (final.astype(F32) + moved).astype(BF16)
        state = passed_along(sent, "seq", 1)
    return state


def grad_from_after(first, trans):
    grad = None
    for _ in range(lax.axis_size("seq") - 1):
        sent = first
        if grad is not None:
            moved = jnp.einsum("mhji,mhjv->mhiv", trans, grad.astype(F32), precision=BEST)
            sent = (first.astype(F32) + moved).astype(BF16)
        grad = passed_along(sent, "seq", -1)
    return grad


def rms_unit(values):
    return values * lax.rsqrt(jnp.mean(values * values, axis=-1, keepdims=True) + 1e-05)


def rms_back(values, gain, d_out):
    inv = lax.rsqrt(jnp.mean(values * values, axis=-1, keepdims=True) + 1e-05)
    unit = values * inv
    d_unit = d_out * gain
    d_values = inv * (d_unit - unit * jnp.mean(d_unit * unit, axis=-1, keepdims=True))
    return d_values, d_out * unit


def mat(left, right):
    return lax.dot_general(left, right, (((2,), (0,)), ((), ())), preferred_element_type=F32)


def mat_t(left, right):
    return lax.dot_general(left, right, (((2,), (1,)), ((), ())), preferred_element_type=F32)


def grad_of(left, right):
    left = left.reshape(-1, left.shape[2])
    right = right.reshape(-1, right.shape[2])
    part = lax.dot_general(left, right, (((0,), (0,)), ((), ())), preferred_element_type=F32)
    return part.astype(BF16)


def scatter_grad(grad):
    return lax.psum_scatter(grad, SEQ_FSDP, scatter_dimension=0, tiled=True).astype(F32)


def per_device(
    block_input,
    cotangent,
    doc_lengths,
    attn_gain,
    w_query,
    w_key,
    w_value,
    w_gate,
    w_alpha,
    w_beta,
    conv_query,
    conv_key,
    conv_value,
    a_log,
    dt_bias,
    head_gain,
    w_out,
    mlp_gain,
    w_ffgate,
    w_ffup,
    w_down,
):
    head_devices = lax.axis_size("head")
    seq_devices = lax.axis_size("seq")
    owners = seq_devices * lax.axis_size("fsdp")
    seq_place = lax.axis_index("seq")
    head_place = lax.axis_index("head")
    tok_count, model = block_input.shape[2:]
    row_count = tok_count // head_devices
    row_first = head_place * row_count
    heads = w_query.shape[1] // DK
    hidden_width = w_ffgate.shape[1]
    qw, vw = heads * DK, heads * DV
    rates_at = 2 * qw + vw

    x_own = block_input[:, 0]
    halo = passed_along(x_own[:, tok_count - PAD :], "seq", 1)
    w_first = jnp.concatenate([w_query, w_key, w_value, w_alpha, w_beta], axis=1)
    w_first = jnp.pad(w_first, ((0, 0), (0, LANES - 2 * heads)))
    w_second = jnp.concatenate([w_gate, w_out.T], axis=1)
    w_third = jnp.stack([w_ffgate.T, w_ffup.T, w_down])
    x_pad = jnp.concatenate([halo, x_own], axis=1).astype(F32)
    h_one = (rms_unit(x_pad) * attn_gain).astype(BF16)
    cot = to_slots(cotangent[:, 0], "head")
    slots = slot_table("head")
    first = GatherWeights(w_first)
    first.swap()
    second = GatherWeights(after(w_second, first.other[0]))
    w_first, h_one, cot = lax.optimization_barrier((first.result(), h_one, cot))

    conv_q = lax.dynamic_slice_in_dim(conv_query, head_place * qw, qw, 1)
    conv_k = lax.dynamic_slice_in_dim(conv_key, head_place * qw, qw, 1)
    conv_v = lax.dynamic_slice_in_dim(conv_value, head_place * vw, vw, 1)
    filters = (conv_q, conv_k, conv_v)
    rates = jnp.stack(
        [
            lax.dynamic_slice_in_dim(a_log, head_place * heads, heads, 0),
            lax.dynamic_slice_in_dim(dt_bias, head_place * heads, heads, 0),
        ]
    )
    params = jnp.pad(rates, ((0, 6), (0, LANES - heads)))
    gain_rows = jnp.broadcast_to(head_gain[None], (8, DV))
    lengths = doc_lengths[:, 0]
    docs = lengths.shape[1]
    counted = jnp.arange(docs)[None, :] < jnp.arange(docs + 1)[:, None]
    ends = jnp.sum(jnp.where(counted[None], lengths[:, None, :], 0), axis=2)
    ends = (ends - seq_place * tok_count).astype(jnp.int32)

    micros = range(block_input.shape[0])
    count = len(micros)
    outputs, forwards, gate_backs, backs = (Shared(count) for _ in range(4))
    x_parts = [
        lax.dynamic_slice_in_dim(x_own[m : m + 1], row_first, row_count, 1).astype(F32)
        for m in micros
    ]
    pres, found, saves, transes = {}, {}, {}, {}
    states_in, gates, outs, statess = {}, {}, {}, {}
    attn, rows_two, x_ones, sums, back_sums, back_rows = {}, {}, {}, {}, {}, {}
    mlp_terms, d_x_ones = {}, {}
    backed, exts, smalls, gain_sums = {}, {}, {}, {}

    def project(m):
        pres[m] = mat(h_one[m : m + 1], w_first)
        return pres[m]

    def local(m, *waits):
        found[m] = run_local(
            ends[m : m + 1], after(pres[m], *waits), filters, params, heads, seq_devices > 2
        )
        saves[m] = tuple(found[m][:7])
        transes[m] = found[m][8] if seq_devices > 2 else None
        states_in[m] = state_from_before(found[m][7], transes[m])
        return found[m][5]

    def project_gate(m):
        gates[m] = mat(h_one[m : m + 1], w_g)
        return gates[m]

    def output(m, *waits):
        outs[m], statess[m], keep, give = run_output(
            outputs,
            m,
            slots,
            after(states_in[m], *waits),
            saves[m],
            gates[m],
            gain_rows,
            w_second,
        )
        attn[m] = Scatter(keep, give, "head")
        return keep

    def to_feed_forward(m, summed):
        x_ones[m] = x_parts[m] + summed
        rows_two[m] = Gather((rms_unit(x_ones[m]) * mlp_gain).astype(BF16), "head")

    def feed_forward(m, halves, *waits):
        low, high = halves
        keep, give = run_feed_forward(forwards, m, (after(low, *waits), high), cot, w_third)
        sums[m] = Scatter(keep, give, "head")
        return keep

    def to_gate_back(m, summed):
        d_norm, terms = rms_back(x_ones[m], mlp_gain, summed)
        mlp_terms[m] = jnp.sum(terms, axis=(0, 1))
        d_x_ones[m] = cot[m : m + 1, :row_count].astype(F32) + d_norm
        back_rows[m] = Gather(d_x_ones[m].astype(BF16), "head")

    def gate_back(m, halves, *waits):
        low, high = halves
        d_out, added, grad_first, gain_sum = run_gate_back(
            gate_backs,
            m,
            slots,
            (after(low, *waits), high),
            outs[m],
            gates[m],
            gain_rows,
            saves[m],
            w_second,
        )
        gain_sums[m] = gain_sum
        backed[m] = (d_out, added, grad_from_after(grad_first, transes[m]))
        return gain_sum

    def back(m, *waits):
        d_out, added, grad_incoming = backed[m]
        exts[m], smalls[m] = run_back(
            backs,
            m,
            pres[m],
            filters,
            saves[m],
            statess[m],
            added,
            after(grad_incoming, *waits),
            d_out,
        )
        return smalls[m]

    project(0)
    done = local(0)
    second.swap(done)
    w_third = lax.all_gather(after(w_third, *second.got), "fsdp", axis=0)
    project(1)
    done = local(1, done)
    w_second = second.result(done)
    w_g = w_second[:, :vw]
    project_gate(0)
    done = output(0, done)
    project(2)
    done = local(2, done)
    attn[0].advance(done)
    project_gate(1)
    done = output(1, done, attn[0].sent)
    to_feed_forward(0, attn[0].finish(done))
    project_gate(2)
    done = output(2, done, rows_two[0].sent)
    attn[1].advance(done)
    rows_two[0].advance(attn[1].sent)
    attn[2].advance(rows_two[0].sent)
    done = feed_forward(0, rows_two[0].finish(attn[2].sent))
    to_feed_forward(1, attn[1].finish(done))
    to_feed_forward(2, attn[2].finish(rows_two[1].sent))
    sums[0].advance(rows_two[2].sent)
    rows_two[1].advance(sums[0].sent)
    done = feed_forward(1, rows_two[1].finish(rows_two[1].sent))
    rows_two[2].advance(done)
    sums[1].advance(rows_two[2].sent)
    to_gate_back(0, sums[0].finish(sums[1].sent))
    done = feed_forward(2, rows_two[2].finish(back_rows[0].sent))
    out_keep, out_give, h_two, hid, d_ffg, d_ffu = forwards.arrays
    grad_gate = grad_of(after(d_ffg, done), h_two)
    sums[2].advance(grad_gate)
    back_rows[0].advance(sums[2].sent)
    grad_up = grad_of(after(d_ffu, back_rows[0].sent), h_two)
    to_gate_back(1, sums[1].finish(grad_up))
    grad_down = grad_of(after(hid, back_rows[1].sent), cot)
    done = gate_back(0, back_rows[0].finish(grad_down))
    back_rows[1].advance(done)
    to_gate_back(2, sums[2].finish(back_rows[1].sent))
    ff_grads = jnp.stack([after(grad_gate, back_rows[2].sent), grad_up, grad_down])
    ff_grads = ff_grads.reshape(3, hidden_width, owners, -1)
    ff_grads = jnp.transpose(ff_grads, (2, 0, 1, 3))
    ff_shard = scatter_grad(ff_grads)[0]
    done = gate_back(1, back_rows[1].finish(ff_grads))
    back_rows[2].advance(done)
    done = back(0, back_rows[2].sent)
    done = gate_back(2, back_rows[2].finish(done), backed[1][2])
    out_sum = Scatter(after(out_keep, done), out_give, "head")
    d_gates, d_attn_rows = gate_backs.arrays
    side_grads = jnp.concatenate(
        [grad_of(h_one, d_gates), grad_of(d_attn_rows, outputs.arrays[0])], axis=1
    )
    side = Reduce(side_grads)
    dx_parts, attn_terms, d_h_sums = {}, {}, {}

    def to_input(m, *waits):
        d_ext, d_gate = exts[m], d_gates[m : m + 1]
        rims = after(passed_along(d_ext[:, :PAD], "seq", -1), *waits)
        d_h_one = mat_t(d_ext[:, PAD:], w_first) + mat_t(d_gate[:, PAD:], w_g)
        d_rim = mat_t(rims, w_first)
        d_h_one = d_h_one + jnp.pad(d_rim, ((0, 0), (tok_count - PAD, 0), (0, 0)))
        unit_own = rms_unit(x_own[m : m + 1].astype(F32))
        attn_terms[m] = jnp.sum(d_h_one * unit_own, axis=(0, 1))
        d_h_one = to_slots(d_h_one.astype(BF16), "head")
        half = tok_count // 2
        d_h_sums[m] = Scatter(d_h_one[:, :half], d_h_one[:, half:], "head")

    def to_end(m, summed):
        d_first, _ = rms_back(x_parts[m], attn_gain, summed)
        dx_parts[m] = d_x_ones[m] + d_first

    done = back(1, done, side.sent, backed[2][2], out_sum.sent)
    to_input(0, done)
    to_input(1, d_h_sums[0].sent)
    out_sum.advance(d_h_sums[1].sent)
    side.spread(out_sum.sent)
    d_h_sums[0].advance(*side.gives)
    done = back(2, done, *side.gives, d_h_sums[0].sent, ff_shard)
    x_all = jnp.concatenate([x_ones[m] for m in micros])
    block_output = (x_all + out_sum.finish(done)).astype(BF16)
    mix_grad = grad_of(h_one, backs.arrays[0])
    mix = [Reduce(mix_grad[:, : 2 * qw]), Reduce(mix_grad[:, 2 * qw :])]
    to_input(2, mix[0].sent, mix[1].sent)
    d_h_sums[1].advance(d_h_sums[2].sent)

    small = sum(jnp.sum(one, axis=0) for one in smalls.values())
    rate_sums = small[:2, rates_at : rates_at + heads]
    taps = small[:KCONV]
    sizes = (conv_query.shape[1], conv_key.shape[1], conv_value.shape[1])
    widened = [
        lax.dynamic_update_slice_in_dim(
            jnp.zeros((KCONV, size), F32), taps[:, at : at + width], head_place * width, 1
        )
        for size, at, width in zip(sizes, (0, qw, 2 * qw), (qw, qw, vw))
    ]
    widened_rates = lax.dynamic_update_slice_in_dim(
        jnp.zeros((2, a_log.shape[0]), F32), rate_sums, head_place * heads, 1
    )
    gain_sum = sum(jnp.sum(one[:, 0], axis=0) for one in gain_sums.values())
    pieces = [sum(attn_terms.values()), sum(mlp_terms.values()), gain_sum] + widened + [widened_rates]
    packed = jnp.concatenate([piece.reshape(-1) for piece in pieces])
    length = packed.shape[0]
    packed = jnp.pad(packed, (0, -length % 1024)).reshape(-1, LANES)
    small_sum = SmallSum(packed)
    small_sum.step()
    side_shard = side.finish(small_sum.value)
    to_end(0, d_h_sums[0].finish(small_sum.value))
    ff_shard = [ff_shard[0].T, ff_shard[1].T, ff_shard[2]]
    mix[0].spread(side_shard, block_output, dx_parts[0])
    d_h_sums[2].advance(*mix[0].gives)
    small_sum.step(*mix[0].gives)
    to_end(1, d_h_sums[1].finish(small_sum.value))
    mix[1].spread(small_sum.value, *ff_shard, dx_parts[1])
    small_sum.step(*mix[1].gives)
    to_end(2, d_h_sums[2].finish(small_sum.value))
    input_grad = jnp.concatenate([dx_parts[m] for m in micros])
    total = mix[0].finish(input_grad)
    shard_mix = jnp.concatenate([total, mix[1].finish(total)], axis=1)
    packed = small_sum.finish().reshape(-1)
    totals, at = [], 0
    for piece in pieces:
        totals.append(packed[at : at + piece.size].reshape(piece.shape))
        at += piece.size
    tot_attn, tot_mlp, tot_head, tot_cq, tot_ck, tot_cv, tot_rates = totals
    return (
        block_output[:, None],
        input_grad[:, None],
        shard_mix[:, :qw],
        shard_mix[:, qw : 2 * qw],
        shard_mix[:, 2 * qw : rates_at],
        side_shard[:, :vw],
        shard_mix[:, rates_at : rates_at + heads],
        shard_mix[:, rates_at + heads : rates_at + 2 * heads],
        side_shard[:, vw:].T,
        ff_shard[0],
        ff_shard[1],
        ff_shard[2],
        tot_attn,
        tot_mlp,
        tot_head,
        tot_cq,
        tot_ck,
        tot_cv,
        tot_rates[0],
        tot_rates[1],
    )


def solution(mesh):
    rows_by_fsdp = P("fsdp", "head")
    cols_by_fsdp = P("head", "fsdp")
    tokens = P(None, "fsdp", "seq", None)
    return jax.shard_map(
        per_device,
        mesh=mesh,
        in_specs=(
            (tokens, tokens, P(None, "fsdp", None), P())
            + (rows_by_fsdp,) * 6
            + (P(),) * 6
            + (cols_by_fsdp, P(), rows_by_fsdp, rows_by_fsdp, cols_by_fsdp)
        ),
        out_specs=(
            (P(None, "fsdp", ("seq", "head"), None),) * 2
            + (P(SEQ_FSDP, "head"),) * 6
            + (P("head", SEQ_FSDP), P(SEQ_FSDP, "head"), P(SEQ_FSDP, "head"))
            + (P("head", SEQ_FSDP),)
            + (P(),) * 8
        ),
        check_vma=False,
    )
```
